32 devices in a mesh: seq: 2 (over core), fsdp: 16 (over z, y, x).
Axes of the slice: x: 2, y: 2, z: 4, core: 2. Of those that a mesh axis runs over, the one named last changes fastest.
Arguments:
- byte_stream: bfloat16 [16, 768, 768], P('fsdp', 'seq'), may hold values from -6 to 6
- latents: bfloat16 [16, 3072, 1280], P('fsdp', 'seq')
- out_grad: bfloat16 [16, 3072, 1280], P('fsdp', 'seq'), may hold values from -6 to 6
- doc_lengths: int32 [16, 9], P('fsdp'), may hold values from 1 to 384, 768 in all within a row
- slot_ids: int32 [16, 12], P('fsdp'), may hold values from 0 to 11, each once within a row
- byte_gain: bfloat16 [768], P('fsdp'), may hold values from 0.25 to 1.75
- byte_shift: bfloat16 [768], P('fsdp'), may hold values from -1.5 to 1.5
- latent_gain: bfloat16 [1280], P('fsdp'), may hold values from 0.25 to 1.75
- latent_shift: bfloat16 [1280], P('fsdp'), may hold values from -1.5 to 1.5
- mlp_gain: bfloat16 [1280], P('fsdp'), may hold values from 0.25 to 1.75
- mlp_shift: bfloat16 [1280], P('fsdp'), may hold values from -1.5 to 1.5
- w_query: bfloat16 [1280, 256], P('fsdp'), may hold values from -0.15625 to 0.15625
- w_key: bfloat16 [768, 256], P('fsdp'), may hold values from -0.21875 to 0.21875
- w_value: bfloat16 [768, 1280], P('fsdp'), may hold values from -0.21875 to 0.21875
- w_out: bfloat16 [1280, 1280], P('fsdp'), may hold values from -1.5 to 1.5
- w_up: bfloat16 [1280, 1280], P('fsdp'), may hold values from -0.15625 to 0.15625
- up_bias: bfloat16 [1280], P('fsdp'), may hold values from -2.5 to 2.5
- w_down: bfloat16 [1280, 1280], P('fsdp'), may hold values from -0.15625 to 0.15625
- down_bias: bfloat16 [1280], P('fsdp'), may hold values from -1.5 to 1.5
Outputs:
- new_latents: bfloat16 [16, 3072, 1280], P('fsdp', 'seq')
- latent_grad: bfloat16 [16, 3072, 1280], P('fsdp', 'seq')
- byte_grad: bfloat16 [16, 768, 768], P('fsdp', 'seq')
- byte_gain_grad: float32 [768], P('fsdp')
- byte_shift_grad: float32 [768], P('fsdp')
- latent_gain_grad: float32 [1280], P('fsdp')
- latent_shift_grad: float32 [1280], P('fsdp')
- mlp_gain_grad: float32 [1280], P('fsdp')
- mlp_shift_grad: float32 [1280], P('fsdp')
- w_query_grad: float32 [1280, 256], P('fsdp')
- w_key_grad: float32 [768, 256], P('fsdp')
- w_value_grad: float32 [768, 1280], P('fsdp')
- w_out_grad: float32 [1280, 1280], P('fsdp')
- w_up_grad: float32 [1280, 1280], P('fsdp')
- up_bias_grad: float32 [1280], P('fsdp')
- w_down_grad: float32 [1280, 1280], P('fsdp')
- down_bias_grad: float32 [1280], P('fsdp')
- rms_values: float32 [3], replicated
The draws below stay inside these ranges and needn't reach their ends.
Inputs may be any that keep to these rules, and one draw needn't show every extreme that they name: `doc_lengths`: the 9 lengths of a group sum to 768. Each row names every slot once; document d uses slot slot_ids[d] for d < 9, the other slots hold no document.
All inputs are finite; a program needn't handle non-finite values.
Results may differ from the reference program's by a relative error of at most 0.014.
Values may be sent and summed in bfloat16 or wider, within the bound.
No kernel may reach another device: no remote copies, remote signals or barrier semaphores. Data moves between devices by JAX's collectives and lax.ppermute only.
A program may use at most 192 MiB of HBM per device.

```python
import math
from functools import partial
import jax
import jax.numpy as jnp
import numpy as np
from jax import lax

D_BYTE = 768
D_LAT = 1280
FFN = 1280
HEADS = 8
QK = 256
LAT = 256
TOK_DEV = 384
GROUP_BYTES = 768
SLOTS = 12
DOCS = 9
LAT_ROWS = 3072
GROUPS = 16


def draw_latents(key, part):
    key_base, key_rows, key_cols = jax.random.split(key, 3)
    full_shape = (GROUPS, LAT_ROWS, D_LAT)
    group_ramp = 0.6 + 1.2 * jnp.arange(GROUPS, dtype=jnp.float32) / max(GROUPS - 1, 1)
    row_scale = jnp.exp(jax.random.uniform(key_rows, (GROUPS, LAT_ROWS, 1), minval=math.log(0.3), maxval=math.log(3.0)))
    col_scale = jnp.exp(jax.random.uniform(key_cols, (1, 1, D_LAT), minval=math.log(0.5), maxval=math.log(2.0)))
    base_draw = jax.random.normal(key_base, full_shape)
    return (base_draw * row_scale * col_scale * group_ramp[:, None, None]).astype(jnp.bfloat16)


def levels(stream_key, extent, pieces, low, high):
    level, own = 1.0, jax.random.fold_in(stream_key, 6)
    for position, shards_of in pieces:
        draws = jnp.exp(jax.random.uniform(jax.random.fold_in(own, position), (shards_of,), jnp.float32, low / len(pieces), high / len(pieces)))
        level = level * jnp.repeat(draws, extent[position] // shards_of).reshape([-1 if axis == position else 1 for axis in range(len(extent))])
    return level


def length_profile(count, total, reach, lean):
    weights = [(1 << 20) // math.isqrt(rank ** lean) + 1 for rank in range(2, count + 1)]
    rest, holding = total - reach - (count - 1), [1] * (count - 1)
    while rest > 0:
        movable = [i for i in range(count - 1) if holding[i] < reach]
        mass, left = sum([weights[i] for i in movable]), rest
        for i in movable:
            extra = min(reach - holding[i], max(1, left * weights[i] // mass), rest)
            holding[i] = holding[i] + extra
            rest = rest - extra
    return np.array([reach] + holding)


def uneven(key, number_of, total, bound, skew):
    if number_of == 2:
        one = jax.random.randint(key, (), max(1, total - bound), min(bound, total - 1) + 1)
        return jnp.stack([one, total - one])
    tallies = jnp.asarray(length_profile(number_of, total, bound, skew), jnp.int32)
    couples = (number_of - 1) // 2
    giver, sink = tallies[1:1 + 2 * couples:2], tallies[2:2 + 2 * couples:2]
    slack = jnp.minimum(giver - 1, bound - sink)
    passed = jax.random.randint(jax.random.fold_in(key, 1), (couples,), 0, 1 << 20) % (slack + 1)
    tallies = tallies.at[1:1 + 2 * couples:2].set(giver - passed).at[2:2 + 2 * couples:2].set(sink + passed)
    return tallies[jax.random.permutation(jax.random.fold_in(key, 2), number_of)]


def bell_draw(own_key, extent, width, reach, cuts=(), held_as=jnp.bfloat16):
    level = levels(own_key, extent, cuts, -0.22, 0.18) if cuts else 1.0
    values = jax.random.normal(own_key, extent, jnp.float32) * width * level
    return jnp.minimum(jnp.maximum(values, -reach), reach).astype(held_as)


def setup_inputs(seed: int = 0) -> dict:
    seeds = jax.random.split(jax.random.key(seed), 20)
    return {
        "byte_stream": bell_draw(seeds[0], (GROUPS, GROUP_BYTES, D_BYTE), 1.0, 6.0, ((0, 16), (1, 2))),
        "latents": draw_latents(jax.random.fold_in(seeds[19], 71), 0),
        "out_grad": bell_draw(seeds[2], (GROUPS, LAT_ROWS, D_LAT), 1.0, 6.0, ((0, 16), (1, 2))),
        "doc_lengths": jax.vmap(lambda own: uneven(own, DOCS, GROUP_BYTES, TOK_DEV, 2))(jax.random.split(seeds[3], GROUPS)).reshape((GROUPS, DOCS)).astype(jnp.int32),
        "slot_ids": jax.vmap(lambda own: jax.random.permutation(own, SLOTS))(jax.random.split(seeds[4], GROUPS)).reshape((GROUPS, SLOTS)).astype(jnp.int32),
        "byte_gain": jnp.clip(1.0 + 0.15 * jax.random.normal(seeds[5], (D_BYTE,), jnp.float32), 0.25, 1.75).astype(jnp.bfloat16),
        "byte_shift": bell_draw(seeds[6], (D_BYTE,), 0.3, 1.5, ((0, 16),)),
        "latent_gain": jnp.clip(1.0 + 0.15 * jax.random.normal(seeds[7], (D_LAT,), jnp.float32), 0.25, 1.75).astype(jnp.bfloat16),
        "latent_shift": bell_draw(seeds[8], (D_LAT,), 0.3, 1.5, ((0, 16),)),
        "mlp_gain": jnp.clip(1.0 + 0.15 * jax.random.normal(seeds[9], (D_LAT,), jnp.float32), 0.25, 1.75).astype(jnp.bfloat16),
        "mlp_shift": bell_draw(seeds[10], (D_LAT,), 0.3, 1.5, ((0, 16),)),
        "w_query": bell_draw(seeds[11], (D_LAT, QK), D_LAT ** -0.5, 0.15625, ((0, 16),)),
        "w_key": bell_draw(seeds[12], (D_BYTE, QK), D_BYTE ** -0.5, 0.21875, ((0, 16),)),
        "w_value": bell_draw(seeds[13], (D_BYTE, D_LAT), D_BYTE ** -0.5, 0.21875, ((0, 16),)),
        "w_out": bell_draw(seeds[14], (D_LAT, D_LAT), (D_LAT * DOCS // GROUP_BYTES) ** -0.5, 1.5, ((0, 16),)),
        "w_up": bell_draw(seeds[15], (D_LAT, FFN), D_LAT ** -0.5, 0.15625, ((0, 16),)),
        "up_bias": bell_draw(seeds[16], (FFN,), 0.5, 2.5, ((0, 16),)),
        "w_down": bell_draw(seeds[17], (FFN, D_LAT), FFN ** -0.5, 0.15625, ((0, 16),)),
        "down_bias": bell_draw(seeds[18], (D_LAT,), 0.3, 1.5, ((0, 16),)),
    }


EPSILON = 1e-05
NEG_FILL = -1e+30

@jax.custom_vjp
def low(v):
    return lax.optimization_barrier(v.astype(jnp.bfloat16)).astype(jnp.float32)

@jax.custom_vjp
def low_back(v):
    return v

def low_keep(v):
    return (low(v), None)

def low_pass(kept, grad):
    return (grad,)

def back_keep(v):
    return (v, None)

def back_low(kept, grad):
    return (low(grad),)
low.defvjp(low_keep, low_pass)
low_back.defvjp(back_keep, back_low)

def matmul(left, right):
    return jnp.dot(left, right, preferred_element_type=jnp.float32, precision=lax.Precision.HIGHEST)

def layer_norm(values, gain, shift):
    centred = values - lax.optimization_barrier(jnp.mean(values, axis=-1, keepdims=True))
    inverse = lax.rsqrt(lax.optimization_barrier(jnp.mean(centred * centred, axis=-1, keepdims=True)) + EPSILON)
    return centred * inverse * gain + shift

def doc_tables(lengths, slots):
    doc_ends = jnp.cumsum(lengths).astype(jnp.int32)
    positions = jnp.arange(GROUP_BYTES, dtype=jnp.int32)
    doc_index = lax.optimization_barrier(jnp.sum((positions[:, None] >= doc_ends[None, :]).astype(jnp.int32), axis=1)).astype(jnp.int32)
    chosen = slots[:DOCS]
    byte_slot = chosen[doc_index]
    slot_used = lax.optimization_barrier(jnp.sum((chosen[:, None] == jnp.arange(SLOTS, dtype=jnp.int32)[None, :]).astype(jnp.float32), axis=0))
    return (byte_slot, slot_used)

def attend(query_rows, key_rows, value_rows, row_slot, byte_slot):
    block_rows = min(512, LAT_ROWS)
    blocks = LAT_ROWS // block_rows
    key_width = QK // HEADS
    score_scale = 1.0 / math.sqrt(key_width)
    key_split = key_rows.reshape(GROUP_BYTES, HEADS, key_width)
    value_split = value_rows.reshape(GROUP_BYTES, HEADS, D_LAT // HEADS)

    def one_block(block_in):
        query_block, slot_block = block_in
        query_split = query_block.reshape(block_rows, HEADS, key_width)
        raw_scores = low_back(jnp.einsum('rhd,bhd->hrb', query_split, key_split, precision=lax.Precision.HIGHEST) * score_scale)
        allowed = (slot_block[:, None] == byte_slot[None, :])[None]
        prob_rows = jax.nn.softmax(jnp.where(allowed, raw_scores, NEG_FILL), axis=-1)
        mixed_out = jnp.einsum('hrb,bhe->rhe', low(prob_rows), value_split, precision=lax.Precision.HIGHEST)
        return mixed_out.reshape(block_rows, D_LAT)
    mixed_rows = lax.map(jax.checkpoint(one_block), (query_rows.reshape(blocks, block_rows, QK), row_slot.reshape(blocks, block_rows)))
    return mixed_rows.reshape(LAT_ROWS, D_LAT)

def group_forward(params, byte_rows, latent_rows, lengths, slots):
    byte_gain, byte_shift, latent_gain, latent_shift, mlp_gain, mlp_shift, w_query, w_key, w_value, w_out, w_up, up_bias, w_down, down_bias = params
    byte_slot, slot_used = doc_tables(lengths, slots)
    row_slot = (jnp.arange(LAT_ROWS, dtype=jnp.int32) // LAT).astype(jnp.int32)
    row_flag = slot_used[row_slot][:, None]
    byte_norm = low(layer_norm(byte_rows, byte_gain, byte_shift))
    key_rows = low(low_back(matmul(byte_norm, w_key)))
    value_rows = low(low_back(matmul(byte_norm, w_value)))
    latent_norm = low(layer_norm(latent_rows, latent_gain, latent_shift))
    query_rows = low(low_back(matmul(latent_norm, w_query)))
    mixed_rows = low(low_back(row_flag * attend(query_rows, key_rows, value_rows, row_slot, byte_slot)))
    attn_out = low_back(matmul(mixed_rows, w_out))
    middle = latent_rows + attn_out
    middle_norm = low(layer_norm(middle, mlp_gain, mlp_shift))
    hidden_pre = low_back(matmul(middle_norm, w_up) + up_bias)
    activated = low(jax.nn.gelu(hidden_pre, approximate=False))
    branch = low_back(matmul(activated, w_down) + down_bias)
    result = middle + branch
    stat_sums = jnp.stack([jnp.sum(row_flag * result * result), jnp.sum(row_flag * attn_out * attn_out), jnp.sum(row_flag * branch * branch)])
    return (result, stat_sums)

def reference(byte_stream, latents, out_grad, doc_lengths, slot_ids, byte_gain, byte_shift, latent_gain, latent_shift, mlp_gain, mlp_shift, w_query, w_key, w_value, w_out, w_up, up_bias, w_down, down_bias):
    floats = tuple((member.astype(jnp.float32) for member in (byte_stream, latents, byte_gain, byte_shift, latent_gain, latent_shift, mlp_gain, mlp_shift, w_query, w_key, w_value, w_out, w_up, up_bias, w_down, down_bias)))

    def forward(byte_all, latent_all, *params):

        def one_group(state_in, group_in):
            byte_rows, latent_rows, lengths, slots = group_in
            result, stat_sums = jax.checkpoint(partial(group_forward, params))(byte_rows, latent_rows, lengths, slots)
            return (state_in, (result, stat_sums))
        scan_end, (results, stats) = lax.scan(one_group, jnp.zeros((), jnp.float32), (byte_all, latent_all, doc_lengths, slot_ids))
        return (results, stats)
    results, backward, stats = jax.vjp(forward, *floats, has_aux=True)
    grads = backward(out_grad.astype(jnp.float32))
    rms_values = jnp.sqrt(lax.optimization_barrier(jnp.sum(stats, axis=0)) / (DOCS * LAT * GROUPS * D_LAT))
    return (results.astype(jnp.bfloat16), grads[1].astype(jnp.bfloat16), grads[0].astype(jnp.bfloat16), grads[2], grads[3], grads[4], grads[5], grads[6], grads[7], grads[8], grads[9], grads[10], grads[11], grads[12], grads[13], grads[14], grads[15], rms_values)
```

```python
import math

import jax
import jax.numpy as jnp
from jax import lax
from jax.experimental import pallas as pl
from jax.experimental.pallas import tpu as pltpu
from jax.sharding import PartitionSpec as P

D_LAT = 1280
D_BYTE = 768
HEADS = 8
QK = 256
LAT = 256
WIN = 128
EPSILON = 1e-05
NEG_FILL = -1e30
KEY_W = QK // HEADS
VAL_W = D_LAT // HEADS
SCALE = 1.0 / math.sqrt(KEY_W)
F32 = jnp.float32
BF16 = jnp.bfloat16


def dot_nn(a, b):
    return lax.dot_general(a, b, (((1,), (0,)), ((), ())), preferred_element_type=F32)


def dot_nt(a, b):
    return lax.dot_general(a, b, (((1,), (1,)), ((), ())), preferred_element_type=F32)


def dot_tn(a, b):
    return lax.dot_general(a, b, (((0,), (0,)), ((), ())), preferred_element_type=F32)


def params(mib=56):
    return pltpu.CompilerParams(
        dimension_semantics=("arbitrary",), vmem_limit_bytes=mib * 1024 * 1024
    )


def norm_parts(v):
    centred = v - jnp.mean(v, axis=-1, keepdims=True)
    inverse = lax.rsqrt(jnp.mean(centred * centred, axis=-1, keepdims=True) + EPSILON)
    return centred * inverse, inverse


def norm_back(upstream, hat, inverse, gain):
    scaled = upstream * gain
    centred = scaled - jnp.mean(scaled, axis=-1, keepdims=True)
    return inverse * (centred - hat * jnp.mean(scaled * hat, axis=-1, keepdims=True))


def colsum(v):
    return jnp.sum(v, axis=0, keepdims=True)


def whole(shape):
    return pl.BlockSpec(shape, lambda i, *_: (0,) * len(shape), pipeline_mode=pl.Buffered(1))


def rows_spec(rows, cols):
    return pl.BlockSpec((rows, cols), lambda i, *_: (i, 0))


def acc_spec(rows, cols):
    return pl.BlockSpec((rows, cols), lambda i, *_: (0, 0))


def cost(flops, nbytes):
    return pl.CostEstimate(flops=int(flops), bytes_accessed=int(nbytes), transcendentals=0)


def byte_forward(byte_rows, w_kv, gain, shift):
    n = byte_rows.shape[0]
    blk = 128
    width = w_kv.shape[1]

    def body(x_ref, w_ref, g_ref, s_ref, low_ref, kv_ref):
        hat, _ = norm_parts(x_ref[...].astype(F32))
        low = (hat * g_ref[...] + s_ref[...]).astype(BF16)
        low_ref[...] = low
        kv_ref[...] = dot_nn(low, w_ref[...]).astype(BF16)

    return pl.pallas_call(
        body,
        name="byte_forward",
        grid=(n // blk,),
        in_specs=[rows_spec(blk, D_BYTE), whole(w_kv.shape), whole(gain.shape), whole(shift.shape)],
        out_specs=[rows_spec(blk, D_BYTE), rows_spec(blk, width)],
        out_shape=[
            jax.ShapeDtypeStruct((n, D_BYTE), BF16),
            jax.ShapeDtypeStruct((n, width), BF16),
        ],
        compiler_params=params(),
        cost_estimate=cost(2 * n * D_BYTE * width, 4e6),
    )(byte_rows, w_kv, gain, shift)


def query_forward(latents, w_q, gain, shift):
    n = latents.shape[0]

    def body(x_ref, w_ref, g_ref, s_ref, low_ref, q_ref):
        hat, _ = norm_parts(x_ref[...].astype(F32))
        low = (hat * g_ref[...] + s_ref[...]).astype(BF16)
        low_ref[...] = low
        q_ref[...] = dot_nn(low, w_ref[...]).astype(BF16)

    return pl.pallas_call(
        body,
        name="query_forward",
        grid=(n // LAT,),
        in_specs=[rows_spec(LAT, D_LAT), whole(w_q.shape), whole(gain.shape), whole(shift.shape)],
        out_specs=[rows_spec(LAT, D_LAT), rows_spec(LAT, QK)],
        out_shape=[jax.ShapeDtypeStruct((n, D_LAT), BF16), jax.ShapeDtypeStruct((n, QK), BF16)],
        compiler_params=params(),
        cost_estimate=cost(2 * n * D_LAT * QK, 1e7),
    )(latents, w_q, gain, shift)


def head_window(h):
    first = (h * VAL_W) // 128 * 128
    return first, h * VAL_W - first


def head_columns(x, low, width):
    col = lax.broadcasted_iota(jnp.int32, (1, x.shape[1]), 1)
    return jnp.where((col >= low) & (col < low + width), x, jnp.zeros((), x.dtype))


def attention_forward(meta, q, k, v):
    n = q.shape[0]
    group = k.shape[0]
    top = min(4, group // WIN)

    def body(meta_ref, q_ref, k_ref, v_ref, out_ref, acc_ref):
        s = pl.program_id(0)
        first = meta_ref[0, s]
        count = meta_ref[1, s]
        lo = meta_ref[2, s]
        hi = meta_ref[3, s]

        @pl.when(count == 0)
        def _():
            out_ref[...] = jnp.zeros(out_ref.shape, BF16)

        def attend(w):
            at = pl.multiple_of(first, WIN)
            width = w * WIN
            pos = at + lax.broadcasted_iota(jnp.int32, (1, width), 1)
            allowed = (pos >= lo) & (pos < hi)
            qs = q_ref[...]
            kw = k_ref[pl.ds(at, width), :]
            acc_ref[...] = jnp.zeros(acc_ref.shape, F32)
            for h in range(HEADS):
                kh = head_columns(kw, h * KEY_W, KEY_W)
                scores = jnp.where(allowed, dot_nt(qs, kh) * SCALE, NEG_FILL)
                e = jnp.exp(scores - jnp.max(scores, axis=-1, keepdims=True))
                p = (e / jnp.sum(e, axis=-1, keepdims=True)).astype(BF16)
                base, off = head_window(h)
                vh = head_columns(v_ref[pl.ds(at, width), base : base + 256], off, VAL_W)
                acc_ref[:, base : base + 256] += dot_nn(p, vh)
            out_ref[...] = acc_ref[...].astype(BF16)

        for w in range(1, top + 1):
            pl.when(count == w)(lambda w=w: attend(w))

    return pl.pallas_call(
        body,
        name="attention_forward",
        grid_spec=pltpu.PrefetchScalarGridSpec(
            num_scalar_prefetch=1,
            grid=(n // LAT,),
            in_specs=[rows_spec(LAT, QK), whole(k.shape), whole(v.shape)],
            out_specs=rows_spec(LAT, D_LAT),
            scratch_shapes=[pltpu.VMEM((LAT, D_LAT), F32)],
        ),
        out_shape=jax.ShapeDtypeStruct((n, D_LAT), BF16),
        compiler_params=params(),
        cost_estimate=cost(4e9, 1e7),
    )(meta, q, k, v)


def attention_backward(meta, q, k, v, grad_mixed):
    n = q.shape[0]
    group = k.shape[0]
    top = min(4, group // WIN)
    steps = n // LAT

    def body(meta_ref, q_ref, k_ref, v_ref, gm_ref, gq_ref, gk_ref, gv_ref, gq_acc, gk_acc, gv_acc):
        s = pl.program_id(0)
        first = meta_ref[0, s]
        count = meta_ref[1, s]
        lo = meta_ref[2, s]
        hi = meta_ref[3, s]

        @pl.when(s == 0)
        def _():
            gk_acc[...] = jnp.zeros(gk_acc.shape, F32)
            gv_acc[...] = jnp.zeros(gv_acc.shape, F32)

        @pl.when(count == 0)
        def _():
            gq_ref[...] = jnp.zeros(gq_ref.shape, BF16)

        def attend(w):
            at = pl.multiple_of(first, WIN)
            width = w * WIN
            pos = at + lax.broadcasted_iota(jnp.int32, (width, 1), 0)
            allowed = (pos >= lo) & (pos < hi)
            qs = q_ref[...]
            kw = k_ref[pl.ds(at, width), :]
            for h in range(HEADS):
                base, off = head_window(h)
                kh = head_columns(kw, h * KEY_W, KEY_W)
                scores = jnp.where(allowed, dot_nt(kh, qs) * SCALE, NEG_FILL)
                e = jnp.exp(scores - jnp.max(scores, axis=0, keepdims=True))
                p = e / jnp.sum(e, axis=0, keepdims=True)
                gm = head_columns(gm_ref[:, base : base + 256], off, VAL_W)
                gp = dot_nt(v_ref[pl.ds(at, width), base : base + 256], gm)
                inner = jnp.sum(p * gp, axis=0, keepdims=True)
                gs = (p * (gp - inner)).astype(BF16)
                gv_acc[pl.ds(at, width), base : base + 256] += dot_nn(p.astype(BF16), gm)
                gk_acc[pl.ds(at, width), :] += dot_nn(gs, head_columns(qs, h * KEY_W, KEY_W))
                part = dot_tn(gs, kh)
                if h == 0:
                    gq_acc[...] = part
                else:
                    gq_acc[...] += part
            gq_ref[...] = (gq_acc[...] * SCALE).astype(BF16)

        for w in range(1, top + 1):
            pl.when(count == w)(lambda w=w: attend(w))

        @pl.when(s == steps - 1)
        def _():
            gk_ref[...] = (gk_acc[...] * SCALE).astype(BF16)
            gv_ref[...] = gv_acc[...].astype(BF16)

    return pl.pallas_call(
        body,
        name="attention_backward",
        grid_spec=pltpu.PrefetchScalarGridSpec(
            num_scalar_prefetch=1,
            grid=(steps,),
            in_specs=[rows_spec(LAT, QK), whole(k.shape), whole(v.shape), rows_spec(LAT, D_LAT)],
            out_specs=[rows_spec(LAT, QK), acc_spec(*k.shape), acc_spec(*v.shape)],
            scratch_shapes=[
                pltpu.VMEM((LAT, QK), F32),
                pltpu.VMEM(k.shape, F32),
                pltpu.VMEM(v.shape, F32),
            ],
        ),
        out_shape=[
            jax.ShapeDtypeStruct((n, QK), BF16),
            jax.ShapeDtypeStruct(k.shape, BF16),
            jax.ShapeDtypeStruct(v.shape, BF16),
        ],
        compiler_params=params(),
        cost_estimate=cost(1e10, 1e7),
    )(meta, q, k, v, grad_mixed)


ROOT_HALF = 1.0 / math.sqrt(2.0)
ROOT_2PI = 1.0 / math.sqrt(2.0 * math.pi)


def middle_stage(flags, mixed, latents, out_grad, w_out, w_up, w_down, vecs):
    n = mixed.shape[0]

    def body(
        flag_ref, mix_ref, lat_ref, g_ref, wo_ref, wu_ref, wd_ref, vec_ref,
        res_ref, act_ref, low_ref, gh_ref, ga_ref, gmid_ref, gmix_ref, sums_ref,
    ):
        i = pl.program_id(0)
        flag = flag_ref[i].astype(F32)
        mlp_gain = vec_ref[0:1, :]
        mlp_shift = vec_ref[1:2, :]
        up_bias = vec_ref[2:3, :]
        down_bias = vec_ref[3:4, :]
        attn = dot_nn(mix_ref[...], wo_ref[...])
        middle = lat_ref[...].astype(F32) + attn
        hat, inverse = norm_parts(middle)
        low = (hat * mlp_gain + mlp_shift).astype(BF16)
        low_ref[...] = low
        hidden = dot_nn(low, wu_ref[...]) + up_bias
        cdf = 0.5 * (1.0 + lax.erf(hidden * ROOT_HALF))
        pdf = jnp.exp(-0.5 * hidden * hidden) * ROOT_2PI
        act = (hidden * cdf).astype(BF16)
        act_ref[...] = act
        branch = dot_nn(act, wd_ref[...]) + down_bias
        result = middle + branch
        res_ref[...] = result.astype(BF16)
        g_low = g_ref[...]
        g = g_low.astype(F32)
        gh = (dot_nt(g_low, wd_ref[...]) * (cdf + hidden * pdf)).astype(BF16)
        gh_ref[...] = gh
        gmn = dot_nt(gh, wu_ref[...])
        gmid = g + norm_back(gmn, hat, inverse, mlp_gain)
        gmid_ref[...] = gmid
        ga = gmid.astype(BF16)
        ga_ref[...] = ga
        gmix_ref[...] = dot_nt(ga, wo_ref[...]).astype(BF16)

        @pl.when(i == 0)
        def _():
            sums_ref[...] = jnp.zeros(sums_ref.shape, F32)

        sums_ref[0:1, :] += flag * colsum(result * result)
        sums_ref[1:2, :] += flag * colsum(attn * attn)
        sums_ref[2:3, :] += flag * colsum(branch * branch)
        sums_ref[3:4, :] += colsum(g)
        sums_ref[4:5, :] += colsum(gh.astype(F32))
        sums_ref[5:6, :] += colsum(gmn * hat)
        sums_ref[6:7, :] += colsum(gmn)

    low_out = jax.ShapeDtypeStruct((n, D_LAT), BF16)
    blk = rows_spec(LAT, D_LAT)
    return pl.pallas_call(
        body,
        name="middle_stage",
        grid_spec=pltpu.PrefetchScalarGridSpec(
            num_scalar_prefetch=1,
            grid=(n // LAT,),
            in_specs=[blk, blk, blk, whole(w_out.shape), whole(w_up.shape), whole(w_down.shape), whole(vecs.shape)],
            out_specs=[blk] * 7 + [acc_spec(8, D_LAT)],
        ),
        out_shape=[
            low_out, low_out, low_out, low_out, low_out,
            jax.ShapeDtypeStruct((n, D_LAT), F32),
            low_out,
            jax.ShapeDtypeStruct((8, D_LAT), F32),
        ],
        compiler_params=params(60),
        cost_estimate=cost(12 * n * D_LAT * D_LAT, 5e7),
    )(flags, mixed, latents, out_grad, w_out, w_up, w_down, vecs)


def norm_backward_stage(name, grad_rows, weight, rows, gain, extra, blk):
    n, d = rows.shape
    width = grad_rows.shape[1]
    has_extra = extra is not None

    def body(*refs):
        gr_ref, w_ref, x_ref, gain_ref = refs[:4]
        out_ref, sums_ref = refs[-2:]
        up = dot_nt(gr_ref[...], w_ref[...])
        hat, inverse = norm_parts(x_ref[...].astype(F32))
        back = norm_back(up, hat, inverse, gain_ref[...])
        if has_extra:
            back = back + refs[4][...]
        out_ref[...] = back.astype(BF16)

        @pl.when(pl.program_id(0) == 0)
        def _():
            sums_ref[...] = jnp.zeros(sums_ref.shape, F32)

        sums_ref[0:1, :] += colsum(up * hat)
        sums_ref[1:2, :] += colsum(up)

    operands = [grad_rows, weight, rows, gain] + ([extra] if has_extra else [])
    specs = [rows_spec(blk, width), whole(weight.shape), rows_spec(blk, d), whole(gain.shape)]
    return pl.pallas_call(
        body,
        name=name,
        grid=(n // blk,),
        in_specs=specs + ([rows_spec(blk, d)] if has_extra else []),
        out_specs=[rows_spec(blk, d), acc_spec(8, d)],
        out_shape=[jax.ShapeDtypeStruct((n, d), BF16), jax.ShapeDtypeStruct((8, d), F32)],
        compiler_params=params(),
        cost_estimate=cost(2 * n * d * width, 1e7),
    )(*operands)


def xor_pairs(count, bit):
    return [(i, i ^ bit) for i in range(count)]


def turn_pairs(count, plane, by):
    depth = count // plane
    return [(i, ((i // plane + by) % depth) * plane + i % plane) for i in range(count)]


def swap_seq(x):
    return lax.ppermute(x, "seq", [(0, 1), (1, 0)])


def gather_blocks(part):
    turn = lambda x, by: lax.ppermute(x, "fsdp", turn_pairs(16, 4, by))
    flip = lambda x, bit: lax.ppermute(x, "fsdp", xor_pairs(16, bit))
    r = part.shape[0]
    deep = jnp.concatenate([part] + [turn(part, by) for by in (1, 2, 3)], axis=0)
    by_x = flip(deep, 1)
    by_y = flip(deep, 2)
    far = [flip(by_x[: 2 * r], 2), flip(by_y[2 * r :], 1)]
    return jnp.concatenate([deep, by_x, by_y] + far, axis=0)


def assemble(place, mine, other, r):
    c = mine.shape[1]

    def body(place_ref, mine_ref, other_ref, out_ref, sems):
        z, y, x, core = place_ref[0], place_ref[1], place_ref[2], place_ref[3]
        copies = []
        for t in range(4):
            for k in range(4):
                chip = ((z + 4 - k) % 4) * 4 + (y ^ (t >> 1)) * 2 + (x ^ (t & 1))
                row = pl.multiple_of(chip * r, 16)
                at = (t * 4 + k) * r
                for which, ref in enumerate((mine_ref, other_ref)):
                    col = pl.multiple_of((core ^ which) * c, 128)
                    copies.append(
                        pltpu.make_async_copy(
                            ref.at[pl.ds(at, r), :],
                            out_ref.at[pl.ds(row, r), pl.ds(col, c)],
                            sems.at[len(copies)],
                        )
                    )
        for copy in copies:
            copy.start()
        for copy in copies:
            copy.wait()

    anywhere = pl.BlockSpec(memory_space=pl.ANY)
    return pl.pallas_call(
        body,
        name="assemble",
        in_specs=[pl.BlockSpec(memory_space=pltpu.SMEM), anywhere, anywhere],
        out_specs=anywhere,
        out_shape=jax.ShapeDtypeStruct((16 * r, 2 * c), BF16),
        scratch_shapes=[pltpu.SemaphoreType.DMA((32,))],
        cost_estimate=cost(0, 6e6),
    )(place, mine, other)


def gather_halves(place, part, core):
    if lax.axis_size("fsdp") != 16:
        return lax.all_gather(part, "fsdp", axis=0, tiled=True)
    c = part.shape[1] // 2
    mine = gather_blocks(lax.dynamic_slice_in_dim(part, core * c, c, axis=1))
    return assemble(place, mine, swap_seq(mine), part.shape[0])


def own_sum(kept, arrived):
    return (kept.astype(F32) + arrived.astype(F32)).astype(BF16)


def reduce_halves(grad, place, core):
    c = grad.shape[1] // 2
    count = lax.axis_size("fsdp")
    kept = lax.dynamic_slice_in_dim(grad, core * c, c, axis=1)
    sent = lax.dynamic_slice_in_dim(grad, (1 - core) * c, c, axis=1)
    half = own_sum(kept, swap_seq(sent))
    if count != 16:
        shard = lax.psum_scatter(half, "fsdp", scatter_dimension=0, tiled=True)
    else:
        z, y, x = place[0], place[1], place[2]
        r = grad.shape[0] // 16
        flip = lambda v, bit: lax.ppermute(v, "fsdp", xor_pairs(16, bit))
        pick = lambda v, i, axis: lax.dynamic_index_in_dim(v, i, axis, keepdims=False)
        blocks = half.reshape(4, 2, 2, r, c)
        a, b = blocks[:2], blocks[2:]
        a = own_sum(pick(a, x, 2), flip(pick(a, 1 - x, 2), 1))
        b = own_sum(pick(b, y, 1), flip(pick(b, 1 - y, 1), 2))
        a = own_sum(pick(a, y, 1), flip(pick(a, 1 - y, 1), 2))
        b = own_sum(pick(b, x, 1), flip(pick(b, 1 - x, 1), 1))
        deep = jnp.concatenate([a, b], axis=0)
        total = pick(deep, z, 0).astype(F32)
        for by in (1, 2, 3):
            piece = pick(deep, (z + by) % 4, 0)
            total = total + lax.ppermute(piece, "fsdp", turn_pairs(16, 4, by)).astype(F32)
        shard = total.astype(BF16)
    twin = swap_seq(shard)
    low = jnp.where(core == 0, shard, twin)
    high = jnp.where(core == 0, twin, shard)
    return low.astype(F32), high.astype(F32)


def total_of(values):
    if lax.axis_size("fsdp") != 16:
        return lax.psum(values, ("seq", "fsdp"))
    values = values + swap_seq(values)
    for bit in (1, 2, 4, 8):
        values = values + lax.ppermute(values, "fsdp", xor_pairs(16, bit))
    return values


def shards(
    byte_stream,
    latents,
    out_grad,
    doc_lengths,
    slot_ids,
    byte_gain,
    byte_shift,
    latent_gain,
    latent_shift,
    mlp_gain,
    mlp_shift,
    w_query,
    w_key,
    w_value,
    w_out,
    w_up,
    up_bias,
    w_down,
    down_bias,
):
    seq_count = lax.axis_size("seq")
    fsdp_count = lax.axis_size("fsdp")
    core = lax.axis_index("seq")
    chip = lax.axis_index("fsdp")
    place = jnp.stack([chip // 4, (chip // 2) % 2, chip % 2, core]).astype(jnp.int32)

    byte_part = byte_gain.shape[0]
    lat_part = latent_gain.shape[0]
    vector_row = jnp.concatenate(
        [byte_gain, byte_shift, latent_gain, latent_shift, mlp_gain, mlp_shift, up_bias, down_bias]
    )
    half_k, half_v = QK // 2, D_LAT // 2
    half_kv = half_k + half_v
    kv_order = jnp.concatenate(
        [w_key[:, :half_k], w_value[:, :half_v], w_key[:, half_k:], w_value[:, half_v:]], axis=1
    )
    vector_rows = jnp.pad(vector_row[None, :], ((0, 15), (0, 2 * half_kv - vector_row.shape[0])))
    first = jnp.concatenate([kv_order, vector_rows], axis=0)
    first_full = gather_halves(place, first, core).reshape(fsdp_count, first.shape[0], -1)
    query_full = gather_halves(place, w_query, core)
    out_full = gather_halves(place, w_out, core)
    up_full = gather_halves(place, w_up, core)
    down_full = gather_halves(place, w_down, core)
    kv_full = first_full[:, :byte_part].reshape(fsdp_count * byte_part, -1)
    packed = first_full[:, byte_part].astype(F32)
    vectors, at = [], 0
    for width in (byte_part, byte_part) + (lat_part,) * 6:
        vectors.append(packed[:, at : at + width].reshape(1, -1))
        at += width
    gain_bytes, shift_bytes, gain_latent, shift_latent, gain_mlp, shift_mlp, bias_up, bias_down = vectors
    vecs = jnp.concatenate([gain_mlp, shift_mlp, bias_up, bias_down] + [bias_down] * 4, axis=0)

    lengths = doc_lengths[0]
    docs = lengths.shape[0]
    slots = slot_ids.shape[1] // seq_count
    ends = jnp.cumsum(lengths)
    own_slots = core * slots + jnp.arange(slots, dtype=jnp.int32)
    hit = (slot_ids[0, :docs][None, :] == own_slots[:, None]).astype(jnp.int32)
    lo = jnp.sum(hit * (ends - lengths)[None, :], axis=1)
    hi = jnp.sum(hit * ends[None, :], axis=1)
    used = jnp.sum(hit, axis=1)
    base = lo // WIN * WIN
    meta = jnp.stack([base, used * ((hi - base + WIN - 1) // WIN), lo, hi]).astype(jnp.int32)

    byte_rows = byte_stream[0]
    latent_rows = latents[0]
    grad_low = out_grad[0]
    byte_low, kv_rows = byte_forward(byte_rows, kv_full, gain_bytes, shift_bytes)
    kv_twin = swap_seq(kv_rows)
    kv_all = jnp.concatenate(
        [jnp.where(core == 0, kv_rows, kv_twin), jnp.where(core == 0, kv_twin, kv_rows)], axis=0
    )
    key_all = jnp.concatenate([kv_all[:, :half_k], kv_all[:, half_kv : half_kv + half_k]], axis=1)
    value_all = jnp.concatenate([kv_all[:, half_k:half_kv], kv_all[:, half_kv + half_k :]], axis=1)
    latent_low, query_rows = query_forward(latent_rows, query_full, gain_latent, shift_latent)
    mixed = attention_forward(meta, query_rows, key_all, value_all)
    result, act, middle_low, grad_hidden, grad_attn, grad_middle, grad_mixed, sums = middle_stage(
        used, mixed, latent_rows, grad_low, out_full, up_full, down_full, vecs
    )
    squares = total_of(jnp.sum(sums[:3], axis=1))
    valid_cells = float(docs * LAT * fsdp_count * D_LAT)
    rms_values = jnp.sqrt(squares / valid_cells)

    def weight_grad(left, right):
        return reduce_halves(dot_tn(left, right).astype(BF16), place, core)

    grad_w_down = weight_grad(act, grad_low)
    grad_w_up = weight_grad(middle_low, grad_hidden)
    grad_w_out = weight_grad(mixed, grad_attn)
    grad_query, grad_key, grad_value = attention_backward(
        meta, query_rows, key_all, value_all, grad_mixed
    )
    home = byte_rows.shape[0]
    grad_kv = jnp.concatenate(
        [grad_key[:, :half_k], grad_value[:, :half_v], grad_key[:, half_k:], grad_value[:, half_v:]],
        axis=1,
    )
    kept = lax.dynamic_slice_in_dim(grad_kv, core * home, home, axis=0)
    sent = lax.dynamic_slice_in_dim(grad_kv, (1 - core) * home, home, axis=0)
    grad_kv_home = own_sum(kept, swap_seq(sent))
    latent_grad, latent_sums = norm_backward_stage(
        "latent_backward", grad_query, query_full, latent_rows, gain_latent, grad_middle, LAT
    )
    byte_grad, byte_sums = norm_backward_stage(
        "byte_backward", grad_kv_home, kv_full, byte_rows, gain_bytes, None, 128
    )
    grad_w_query = weight_grad(latent_low, grad_query)
    grad_w_kv = dot_tn(byte_low, grad_kv_home).astype(BF16)
    by_shard = lambda row: row.reshape(fsdp_count, -1)
    packed_grads = jnp.concatenate(
        [by_shard(byte_sums[0]), by_shard(byte_sums[1]), by_shard(latent_sums[0])]
        + [by_shard(row) for row in (latent_sums[1], sums[5], sums[6], sums[4], sums[3])],
        axis=1,
    ).astype(BF16)
    packed_grads = jnp.pad(
        packed_grads[:, None, :], ((0, 0), (0, 15), (0, 2 * half_kv - packed_grads.shape[1]))
    )
    first_grads = jnp.concatenate(
        [grad_w_kv.reshape(fsdp_count, byte_part, -1), packed_grads], axis=1
    ).reshape(-1, 2 * half_kv)
    low, high = reduce_halves(first_grads, place, core)
    small = jnp.concatenate([low[byte_part], high[byte_part]])
    pieces, at = [], 0
    for width in (byte_part, byte_part) + (lat_part,) * 6:
        pieces.append(small[at : at + width])
        at += width
    side = lambda pair: jnp.concatenate(pair, axis=1)
    grad_w_key = side((low[:byte_part, :half_k], high[:byte_part, :half_k]))
    grad_w_value = side((low[:byte_part, half_k:], high[:byte_part, half_k:]))
    return (
        result[None],
        latent_grad[None],
        byte_grad[None],
        pieces[0],
        pieces[1],
        pieces[2],
        pieces[3],
        pieces[4],
        pieces[5],
        side(grad_w_query),
        grad_w_key,
        grad_w_value,
        side(grad_w_out),
        side(grad_w_up),
        pieces[6],
        side(grad_w_down),
        pieces[7],
        rms_values,
    )


def solution(mesh):
    rows = P("fsdp", "seq", None)
    vec = P("fsdp")
    mat = P("fsdp", None)
    in_specs = (rows,) * 3 + (mat,) * 2 + (vec,) * 6 + (mat,) * 5 + (vec, mat, vec)
    out_specs = (rows,) * 3 + (vec,) * 6 + (mat,) * 5 + (vec, mat, vec, P())
    return jax.shard_map(shards, mesh=mesh, in_specs=in_specs, out_specs=out_specs, check_vma=False)
```

```python
import math

import jax
import jax.numpy as jnp
from jax import lax
from jax.experimental import pallas as pl
from jax.experimental.pallas import tpu as pltpu
from jax.sharding import PartitionSpec as P

D_LAT = 1280
D_BYTE = 768
HEADS = 8
QK = 256
LAT = 256
WIN = 128
EPSILON = 1e-05
NEG_FILL = -1e30
KEY_W = QK // HEADS
VAL_W = D_LAT // HEADS
SCALE = 1.0 / math.sqrt(KEY_W)
F32 = jnp.float32
BF16 = jnp.bfloat16


def dot_nn(a, b):
    return lax.dot_general(a, b, (((1,), (0,)), ((), ())), preferred_element_type=F32)


def dot_nt(a, b):
    return lax.dot_general(a, b, (((1,), (1,)), ((), ())), preferred_element_type=F32)


def dot_tn(a, b):
    return lax.dot_general(a, b, (((0,), (0,)), ((), ())), preferred_element_type=F32)


def params(mib=56):
    return pltpu.CompilerParams(
        dimension_semantics=("arbitrary",), vmem_limit_bytes=mib * 1024 * 1024
    )


def norm_parts(v):
    centred = v - jnp.mean(v, axis=-1, keepdims=True)
    inverse = lax.rsqrt(jnp.mean(centred * centred, axis=-1, keepdims=True) + EPSILON)
    return centred * inverse, inverse


def norm_back(upstream, hat, inverse, gain):
    scaled = upstream * gain
    centred = scaled - jnp.mean(scaled, axis=-1, keepdims=True)
    return inverse * (centred - hat * jnp.mean(scaled * hat, axis=-1, keepdims=True))


def colsum(v):
    return jnp.sum(v, axis=0, keepdims=True)


def whole(shape):
    return pl.BlockSpec(shape, lambda i, *_: (0,) * len(shape), pipeline_mode=pl.Buffered(1))


def rows_spec(rows, cols):
    return pl.BlockSpec((rows, cols), lambda i, *_: (i, 0))


def acc_spec(rows, cols):
    return pl.BlockSpec((rows, cols), lambda i, *_: (0, 0))


def cost(flops, nbytes):
    return pl.CostEstimate(flops=int(flops), bytes_accessed=int(nbytes), transcendentals=0)


def byte_forward(byte_rows, w_kv, gain, shift):
    n = byte_rows.shape[0]
    blk = 128
    width = w_kv.shape[1]

    def body(x_ref, w_ref, g_ref, s_ref, low_ref, kv_ref):
        hat, _ = norm_parts(x_ref[...].astype(F32))
        low = (hat * g_ref[...] + s_ref[...]).astype(BF16)
        low_ref[...] = low
        kv_ref[...] = dot_nn(low, w_ref[...]).astype(BF16)

    return pl.pallas_call(
        body,
        name="byte_forward",
        grid=(n // blk,),
        in_specs=[rows_spec(blk, D_BYTE), whole(w_kv.shape), whole(gain.shape), whole(shift.shape)],
        out_specs=[rows_spec(blk, D_BYTE), rows_spec(blk, width)],
        out_shape=[
            jax.ShapeDtypeStruct((n, D_BYTE), BF16),
            jax.ShapeDtypeStruct((n, width), BF16),
        ],
        compiler_params=params(),
        cost_estimate=cost(2 * n * D_BYTE * width, 4e6),
    )(byte_rows, w_kv, gain, shift)


def query_forward(latents, w_q, gain, shift):
    n = latents.shape[0]

    def body(x_ref, w_ref, g_ref, s_ref, low_ref, q_ref):
        hat, _ = norm_parts(x_ref[...].astype(F32))
        low = (hat * g_ref[...] + s_ref[...]).astype(BF16)
        low_ref[...] = low
        q_ref[...] = dot_nn(low, w_ref[...]).astype(BF16)

    return pl.pallas_call(
        body,
        name="query_forward",
        grid=(n // LAT,),
        in_specs=[rows_spec(LAT, D_LAT), whole(w_q.shape), whole(gain.shape), whole(shift.shape)],
        out_specs=[rows_spec(LAT, D_LAT), rows_spec(LAT, QK)],
        out_shape=[jax.ShapeDtypeStruct((n, D_LAT), BF16), jax.ShapeDtypeStruct((n, QK), BF16)],
        compiler_params=params(),
        cost_estimate=cost(2 * n * D_LAT * QK, 1e7),
    )(latents, w_q, gain, shift)


def head_window(h):
    first = (h * VAL_W) // 128 * 128
    return first, h * VAL_W - first


def head_columns(x, low, width):
    col = lax.broadcasted_iota(jnp.int32, (1, x.shape[1]), 1)
    return jnp.where((col >= low) & (col < low + width), x, jnp.zeros((), x.dtype))


def attention_forward(meta, q, k, v):
    n = q.shape[0]
    group = k.shape[0]
    top = min(4, group // WIN)

    def body(meta_ref, q_ref, k_ref, v_ref, out_ref, acc_ref):
        s = pl.program_id(0)
        first = meta_ref[0, s]
        count = meta_ref[1, s]
        lo = meta_ref[2, s]
        hi = meta_ref[3, s]

        @pl.when(count == 0)
        def _():
            out_ref[...] = jnp.zeros(out_ref.shape, BF16)

        def attend(w):
            at = pl.multiple_of(first, WIN)
            width = w * WIN
            pos = at + lax.broadcasted_iota(jnp.int32, (1, width), 1)
            allowed = (pos >= lo) & (pos < hi)
            qs = q_ref[...]
            kw = k_ref[pl.ds(at, width), :]
            acc_ref[...] = jnp.zeros(acc_ref.shape, F32)
            for h in range(HEADS):
                kh = head_columns(kw, h * KEY_W, KEY_W)
                scores = jnp.where(allowed, dot_nt(qs, kh) * SCALE, NEG_FILL)
                e = jnp.exp(scores - jnp.max(scores, axis=-1, keepdims=True))
                p = (e / jnp.sum(e, axis=-1, keepdims=True)).astype(BF16)
                base, off = head_window(h)
                vh = head_columns(v_ref[pl.ds(at, width), base : base + 256], off, VAL_W)
                acc_ref[:, base : base + 256] += dot_nn(p, vh)
            out_ref[...] = acc_ref[...].astype(BF16)

        for w in range(1, top + 1):
            pl.when(count == w)(lambda w=w: attend(w))

    return pl.pallas_call(
        body,
        name="attention_forward",
        grid_spec=pltpu.PrefetchScalarGridSpec(
            num_scalar_prefetch=1,
            grid=(n // LAT,),
            in_specs=[rows_spec(LAT, QK), whole(k.shape), whole(v.shape)],
            out_specs=rows_spec(LAT, D_LAT),
            scratch_shapes=[pltpu.VMEM((LAT, D_LAT), F32)],
        ),
        out_shape=jax.ShapeDtypeStruct((n, D_LAT), BF16),
        compiler_params=params(),
        cost_estimate=cost(4e9, 1e7),
    )(meta, q, k, v)


def attention_backward(meta, q, k, v, grad_mixed):
    n = q.shape[0]
    group = k.shape[0]
    top = min(4, group // WIN)
    steps = n // LAT

    def body(meta_ref, q_ref, k_ref, v_ref, gm_ref, gq_ref, gk_ref, gv_ref, gq_acc, gk_acc, gv_acc):
        s = pl.program_id(0)
        first = meta_ref[0, s]
        count = meta_ref[1, s]
        lo = meta_ref[2, s]
        hi = meta_ref[3, s]

        @pl.when(s == 0)
        def _():
            gk_acc[...] = jnp.zeros(gk_acc.shape, F32)
            gv_acc[...] = jnp.zeros(gv_acc.shape, F32)

        @pl.when(count == 0)
        def _():
            gq_ref[...] = jnp.zeros(gq_ref.shape, BF16)

        def attend(w):
            at = pl.multiple_of(first, WIN)
            width = w * WIN
            pos = at + lax.broadcasted_iota(jnp.int32, (width, 1), 0)
            allowed = (pos >= lo) & (pos < hi)
            qs = q_ref[...]
            kw = k_ref[pl.ds(at, width), :]
            for h in range(HEADS):
                base, off = head_window(h)
                kh = head_columns(kw, h * KEY_W, KEY_W)
                scores = jnp.where(allowed, dot_nt(kh, qs) * SCALE, NEG_FILL)
                e = jnp.exp(scores - jnp.max(scores, axis=0, keepdims=True))
                p = e / jnp.sum(e, axis=0, keepdims=True)
                gm = head_columns(gm_ref[:, base : base + 256], off, VAL_W)
                gp = dot_nt(v_ref[pl.ds(at, width), base : base + 256], gm)
                inner = jnp.sum(p * gp, axis=0, keepdims=True)
                gs = (p * (gp - inner)).astype(BF16)
                gv_acc[pl.ds(at, width), base : base + 256] += dot_nn(p.astype(BF16), gm)
                gk_acc[pl.ds(at, width), :] += dot_nn(gs, head_columns(qs, h * KEY_W, KEY_W))
                part = dot_tn(gs, kh)
                if h == 0:
                    gq_acc[...] = part
                else:
                    gq_acc[...] += part
            gq_ref[...] = (gq_acc[...] * SCALE).astype(BF16)

        for w in range(1, top + 1):
            pl.when(count == w)(lambda w=w: attend(w))

        @pl.when(s == steps - 1)
        def _():
            gk_ref[...] = (gk_acc[...] * SCALE).astype(BF16)
            gv_ref[...] = gv_acc[...].astype(BF16)

    return pl.pallas_call(
        body,
        name="attention_backward",
        grid_spec=pltpu.PrefetchScalarGridSpec(
            num_scalar_prefetch=1,
            grid=(steps,),
            in_specs=[rows_spec(LAT, QK), whole(k.shape), whole(v.shape), rows_spec(LAT, D_LAT)],
            out_specs=[rows_spec(LAT, QK), acc_spec(*k.shape), acc_spec(*v.shape)],
            scratch_shapes=[
                pltpu.VMEM((LAT, QK), F32),
                pltpu.VMEM(k.shape, F32),
                pltpu.VMEM(v.shape, F32),
            ],
        ),
        out_shape=[
            jax.ShapeDtypeStruct((n, QK), BF16),
            jax.ShapeDtypeStruct(k.shape, BF16),
            jax.ShapeDtypeStruct(v.shape, BF16),
        ],
        compiler_params=params(),
        cost_estimate=cost(1e10, 1e7),
    )(meta, q, k, v, grad_mixed)


ROOT_HALF = 1.0 / math.sqrt(2.0)
ROOT_2PI = 1.0 / math.sqrt(2.0 * math.pi)


def middle_stage(flags, mixed, latents, out_grad, w_out, w_up, w_down, vecs):
    n = mixed.shape[0]

    def body(
        flag_ref, mix_ref, lat_ref, g_ref, wo_ref, wu_ref, wd_ref, vec_ref,
        res_ref, act_ref, low_ref, gh_ref, ga_ref, gmid_ref, gmix_ref, sums_ref,
    ):
        i = pl.program_id(0)
        flag = flag_ref[i].astype(F32)
        mlp_gain = vec_ref[0:1, :]
        mlp_shift = vec_ref[1:2, :]
        up_bias = vec_ref[2:3, :]
        down_bias = vec_ref[3:4, :]
        attn = dot_nn(mix_ref[...], wo_ref[...])
        middle = lat_ref[...].astype(F32) + attn
        hat, inverse = norm_parts(middle)
        low = (hat * mlp_gain + mlp_shift).astype(BF16)
        low_ref[...] = low
        hidden = dot_nn(low, wu_ref[...]) + up_bias
        cdf = 0.5 * (1.0 + lax.erf(hidden * ROOT_HALF))
        pdf = jnp.exp(-0.5 * hidden * hidden) * ROOT_2PI
        act = (hidden * cdf).astype(BF16)
        act_ref[...] = act
        branch = dot_nn(act, wd_ref[...]) + down_bias
        result = middle + branch
        res_ref[...] = result.astype(BF16)
        g_low = g_ref[...]
        g = g_low.astype(F32)
        gh = (dot_nt(g_low, wd_ref[...]) * (cdf + hidden * pdf)).astype(BF16)
        gh_ref[...] = gh
        gmn = dot_nt(gh, wu_ref[...])
        gmid = g + norm_back(gmn, hat, inverse, mlp_gain)
        gmid_ref[...] = gmid
        ga = gmid.astype(BF16)
        ga_ref[...] = ga
        gmix_ref[...] = dot_nt(ga, wo_ref[...]).astype(BF16)

        @pl.when(i == 0)
        def _():
            sums_ref[...] = jnp.zeros(sums_ref.shape, F32)

        sums_ref[0:1, :] += flag * colsum(result * result)
        sums_ref[1:2, :] += flag * colsum(attn * attn)
        sums_ref[2:3, :] += flag * colsum(branch * branch)
        sums_ref[3:4, :] += colsum(g)
        sums_ref[4:5, :] += colsum(gh.astype(F32))
        sums_ref[5:6, :] += colsum(gmn * hat)
        sums_ref[6:7, :] += colsum(gmn)

    low_out = jax.ShapeDtypeStruct((n, D_LAT), BF16)
    blk = rows_spec(LAT, D_LAT)
    return pl.pallas_call(
        body,
        name="middle_stage",
        grid_spec=pltpu.PrefetchScalarGridSpec(
            num_scalar_prefetch=1,
            grid=(n // LAT,),
            in_specs=[blk, blk, blk, whole(w_out.shape), whole(w_up.shape), whole(w_down.shape), whole(vecs.shape)],
            out_specs=[blk] * 7 + [acc_spec(8, D_LAT)],
        ),
        out_shape=[
            low_out, low_out, low_out, low_out, low_out,
            jax.ShapeDtypeStruct((n, D_LAT), F32),
            low_out,
            jax.ShapeDtypeStruct((8, D_LAT), F32),
        ],
        compiler_params=params(60),
        cost_estimate=cost(12 * n * D_LAT * D_LAT, 5e7),
    )(flags, mixed, latents, out_grad, w_out, w_up, w_down, vecs)


def norm_backward_stage(name, grad_rows, weight, rows, gain, extra, blk):
    n, d = rows.shape
    width = grad_rows.shape[1]
    has_extra = extra is not None

    def body(*refs):
        gr_ref, w_ref, x_ref, gain_ref = refs[:4]
        out_ref, sums_ref = refs[-2:]
        up = dot_nt(gr_ref[...], w_ref[...])
        hat, inverse = norm_parts(x_ref[...].astype(F32))
        back = norm_back(up, hat, inverse, gain_ref[...])
        if has_extra:
            back = back + refs[4][...]
        out_ref[...] = back.astype(BF16)

        @pl.when(pl.program_id(0) == 0)
        def _():
            sums_ref[...] = jnp.zeros(sums_ref.shape, F32)

        sums_ref[0:1, :] += colsum(up * hat)
        sums_ref[1:2, :] += colsum(up)

    operands = [grad_rows, weight, rows, gain] + ([extra] if has_extra else [])
    specs = [rows_spec(blk, width), whole(weight.shape), rows_spec(blk, d), whole(gain.shape)]
    return pl.pallas_call(
        body,
        name=name,
        grid=(n // blk,),
        in_specs=specs + ([rows_spec(blk, d)] if has_extra else []),
        out_specs=[rows_spec(blk, d), acc_spec(8, d)],
        out_shape=[jax.ShapeDtypeStruct((n, d), BF16), jax.ShapeDtypeStruct((8, d), F32)],
        compiler_params=params(),
        cost_estimate=cost(2 * n * d * width, 1e7),
    )(*operands)


def xor_pairs(count, bit):
    return [(i, i ^ bit) for i in range(count)]


def turn_pairs(count, plane, by):
    depth = count // plane
    return [(i, ((i // plane + by) % depth) * plane + i % plane) for i in range(count)]


def swap_seq(x):
    return lax.ppermute(x, "seq", [(0, 1), (1, 0)])


def stack_deep(pieces):
    r, c = pieces[0].shape

    def body(*refs):
        for k in range(4):
            refs[4][k * r : (k + 1) * r, :] = refs[k][...]

    return pl.pallas_call(
        body,
        name="stack_deep",
        grid=(1,),
        in_specs=[whole((r, c))] * 4,
        out_specs=pl.BlockSpec((4 * r, c), lambda i: (0, 0)),
        out_shape=jax.ShapeDtypeStruct((4 * r, c), BF16),
        compiler_params=params(),
        cost_estimate=cost(0, 16 * r * c),
    )(*pieces)


def order_half(place, deep, by_x, by_y, far):
    r, c = deep.shape[0] // 4, deep.shape[1]

    def body(place_ref, deep_ref, x_ref, y_ref, far_x_ref, far_y_ref, out_ref):
        p = pl.program_id(0)
        z, y, x = place_ref[0], place_ref[1], place_ref[2]
        k = (z + 4 - p // 4) % 4
        flip_y = ((p // 2) % 2) != y
        flip_x = (p % 2) != x

        def put(when, ref, block):
            @pl.when(when)
            def _():
                out_ref[...] = ref[pl.ds(pl.multiple_of(block * r, 16), r), :]

        far = flip_x & flip_y
        put(jnp.logical_not(flip_x) & jnp.logical_not(flip_y), deep_ref, k)
        put(flip_x & jnp.logical_not(flip_y), x_ref, k)
        put(flip_y & jnp.logical_not(flip_x), y_ref, k)
        put(far & (k < 2), far_x_ref, jnp.minimum(k, 1))
        put(far & (k >= 2), far_y_ref, jnp.maximum(k - 2, 0))

    operands = [deep, by_x, by_y] + far
    return pl.pallas_call(
        body,
        name="order_half",
        grid_spec=pltpu.PrefetchScalarGridSpec(
            num_scalar_prefetch=1,
            grid=(16,),
            in_specs=[whole(v.shape) for v in operands],
            out_specs=rows_spec(r, c),
        ),
        out_shape=jax.ShapeDtypeStruct((16 * r, c), BF16),
        compiler_params=params(),
        cost_estimate=cost(0, 64 * r * c),
    )(place, *operands)


def gather_columns(place, part):
    turn = lambda x, by: lax.ppermute(x, "fsdp", turn_pairs(16, 4, by))
    flip = lambda x, bit: lax.ppermute(x, "fsdp", xor_pairs(16, bit))
    r = part.shape[0]
    deep = stack_deep([part] + [turn(part, by) for by in (1, 2, 3)])
    by_x = flip(deep, 1)
    by_y = flip(deep, 2)
    far = [flip(by_x[: 2 * r], 2), flip(by_y[2 * r :], 1)]
    return order_half(place, deep, by_x, by_y, far)


def join_first(place, mine, other, r, kv_rows):
    c = mine.shape[1]
    wide = c - QK // 2

    def body(place_ref, mine_ref, other_ref, kv_ref, q_ref, vec_ref):
        first = place_ref[3] == 0
        a, b = mine_ref[...], other_ref[...]
        low, high = jnp.where(first, a, b), jnp.where(first, b, a)
        kv_ref[:, :wide] = low[:kv_rows, :wide]
        kv_ref[:, wide:] = high[:kv_rows, :wide]
        q_ref[:, : QK // 2] = low[:, wide:]
        q_ref[:, QK // 2 :] = high[:, wide:]
        vec_ref[...] = a[kv_rows : kv_rows + 16, :128].astype(F32)[:8]

    return pl.pallas_call(
        body,
        name="join_first",
        grid_spec=pltpu.PrefetchScalarGridSpec(
            num_scalar_prefetch=1,
            grid=(16,),
            in_specs=[rows_spec(r, c)] * 2,
            out_specs=[rows_spec(kv_rows, 2 * wide), rows_spec(r, QK), rows_spec(8, 128)],
        ),
        out_shape=[
            jax.ShapeDtypeStruct((16 * kv_rows, 2 * wide), BF16),
            jax.ShapeDtypeStruct((16 * r, QK), BF16),
            jax.ShapeDtypeStruct((16 * 8, 128), F32),
        ],
        compiler_params=params(),
        cost_estimate=cost(0, 128 * r * c),
    )(place, mine, other)


def join_squares(place, mine, other, count):
    n, c = mine.shape
    w = c // count
    blk = n // 8

    def body(place_ref, mine_ref, other_ref, *outs):
        first = place_ref[3] == 0
        for m, out_ref in enumerate(outs):
            a = mine_ref[:, m * w : (m + 1) * w]
            b = other_ref[:, m * w : (m + 1) * w]
            out_ref[:, :w] = jnp.where(first, a, b)
            out_ref[:, w:] = jnp.where(first, b, a)

    return pl.pallas_call(
        body,
        name="join_squares",
        grid_spec=pltpu.PrefetchScalarGridSpec(
            num_scalar_prefetch=1,
            grid=(8,),
            in_specs=[rows_spec(blk, c)] * 2,
            out_specs=[rows_spec(blk, 2 * w)] * count,
        ),
        out_shape=[jax.ShapeDtypeStruct((n, 2 * w), BF16)] * count,
        compiler_params=params(),
        cost_estimate=cost(0, 8 * n * c),
    )(place, mine, other)


def gather_parameters(place, core, kv_halves, w_query, vectors, squares):
    padded = [jnp.pad(v, (0, 128 - v.shape[0])) for v in vectors]
    table = jnp.stack(padded)
    if lax.axis_size("fsdp") != 16:
        take = lambda v: lax.all_gather(v, "fsdp", axis=0, tiled=True)
        whole_table = take(table).reshape(-1, 8, 128).astype(F32)
        return take(jnp.concatenate(kv_halves, axis=1)), take(w_query), whole_table, [
            take(w) for w in squares
        ]
    r = w_query.shape[0]
    kv_rows, wide = kv_halves[0].shape
    half_q = QK // 2
    kv_part = jnp.where(core == 0, kv_halves[0], kv_halves[1])
    q_part = jnp.where(core == 0, w_query[:, :half_q], w_query[:, half_q:])
    left = jnp.concatenate(
        [kv_part, jnp.pad(table, ((0, r - kv_rows - 8), (0, wide - 128)))], axis=0
    )
    first = gather_columns(place, jnp.concatenate([left, q_part], axis=1))
    half = squares[0].shape[1] // 2
    second = gather_columns(
        place,
        jnp.concatenate(
            [jnp.where(core == 0, w[:, :half], w[:, half:]) for w in squares], axis=1
        ),
    )
    kv_full, query_full, whole_table = join_first(place, first, swap_seq(first), r, kv_rows)
    return kv_full, query_full, whole_table.reshape(16, 8, 128), join_squares(
        place, second, swap_seq(second), len(squares)
    )


def own_sum(kept, arrived):
    return (kept.astype(F32) + arrived.astype(F32)).astype(BF16)


def reduce_halves(grads, place, core):
    c = grads[0].shape[1] // 2
    count = lax.axis_size("fsdp")
    halves = []
    for grad in grads:
        kept = lax.dynamic_slice_in_dim(grad, core * c, c, axis=1)
        sent = lax.dynamic_slice_in_dim(grad, (1 - core) * c, c, axis=1)
        halves.append(own_sum(kept, swap_seq(sent)))
    half = jnp.stack(halves)
    if count != 16:
        shard = lax.psum_scatter(half, "fsdp", scatter_dimension=1, tiled=True)
    else:
        z, y, x = place[0], place[1], place[2]
        m, r = len(grads), half.shape[1] // 16
        flip = lambda v, bit: lax.ppermute(v, "fsdp", xor_pairs(16, bit))
        pick = lambda v, i, axis: lax.dynamic_index_in_dim(v, i, axis, keepdims=False)
        blocks = half.reshape(m, 4, 2, 2, r, c)
        a, b = blocks[:, :2], blocks[:, 2:]
        a = own_sum(pick(a, x, 3), flip(pick(a, 1 - x, 3), 1))
        b = own_sum(pick(b, y, 2), flip(pick(b, 1 - y, 2), 2))
        a = own_sum(pick(a, y, 2), flip(pick(a, 1 - y, 2), 2))
        b = own_sum(pick(b, x, 2), flip(pick(b, 1 - x, 2), 1))
        deep = jnp.concatenate([a, b], axis=1)
        total = pick(deep, z, 1).astype(F32)
        for by in (1, 2, 3):
            piece = pick(deep, (z + by) % 4, 1)
            total = total + lax.ppermute(piece, "fsdp", turn_pairs(16, 4, by)).astype(F32)
        shard = total.astype(BF16)
    twin = swap_seq(shard)
    low = jnp.where(core == 0, shard, twin).astype(F32)
    high = jnp.where(core == 0, twin, shard).astype(F32)
    return [(low[m], high[m]) for m in range(len(grads))]


def total_of(values):
    if lax.axis_size("fsdp") != 16:
        return lax.psum(values, ("seq", "fsdp"))
    values = values + swap_seq(values)
    for bit in (1, 2, 4, 8):
        values = values + lax.ppermute(values, "fsdp", xor_pairs(16, bit))
    return values


def shards(
    byte_stream,
    latents,
    out_grad,
    doc_lengths,
    slot_ids,
    byte_gain,
    byte_shift,
    latent_gain,
    latent_shift,
    mlp_gain,
    mlp_shift,
    w_query,
    w_key,
    w_value,
    w_out,
    w_up,
    up_bias,
    w_down,
    down_bias,
):
    seq_count = lax.axis_size("seq")
    fsdp_count = lax.axis_size("fsdp")
    core = lax.axis_index("seq")
    chip = lax.axis_index("fsdp")
    place = jnp.stack([chip // 4, (chip // 2) % 2, chip % 2, core]).astype(jnp.int32)

    byte_part = byte_gain.shape[0]
    lat_part = latent_gain.shape[0]
    half_k, half_v = QK // 2, D_LAT // 2
    half_kv = half_k + half_v
    kv_halves = [
        jnp.concatenate([w_key[:, :half_k], w_value[:, :half_v]], axis=1),
        jnp.concatenate([w_key[:, half_k:], w_value[:, half_v:]], axis=1),
    ]
    kv_full, query_full, table, (out_full, up_full, down_full) = gather_parameters(
        place,
        core,
        kv_halves,
        w_query,
        (byte_gain, byte_shift, latent_gain, latent_shift, mlp_gain, mlp_shift, up_bias, down_bias),
        (w_out, w_up, w_down),
    )
    widths = (byte_part, byte_part) + (lat_part,) * 6
    vectors = [table[:, i, :width].reshape(1, -1) for i, width in enumerate(widths)]
    gain_bytes, shift_bytes, gain_latent, shift_latent = vectors[:4]
    bias_down = vectors[7]
    vecs = jnp.concatenate(vectors[4:] + [bias_down] * 4, axis=0)

    lengths = doc_lengths[0]
    docs = lengths.shape[0]
    slots = slot_ids.shape[1] // seq_count
    ends = jnp.cumsum(lengths)
    own_slots = core * slots + jnp.arange(slots, dtype=jnp.int32)
    hit = (slot_ids[0, :docs][None, :] == own_slots[:, None]).astype(jnp.int32)
    lo = jnp.sum(hit * (ends - lengths)[None, :], axis=1)
    hi = jnp.sum(hit * ends[None, :], axis=1)
    used = jnp.sum(hit, axis=1)
    base = lo // WIN * WIN
    meta = jnp.stack([base, used * ((hi - base + WIN - 1) // WIN), lo, hi]).astype(jnp.int32)

    byte_rows = byte_stream[0]
    latent_rows = latents[0]
    grad_low = out_grad[0]
    byte_low, kv_rows = byte_forward(byte_rows, kv_full, gain_bytes, shift_bytes)
    kv_twin = swap_seq(kv_rows)
    kv_all = jnp.concatenate(
        [jnp.where(core == 0, kv_rows, kv_twin), jnp.where(core == 0, kv_twin, kv_rows)], axis=0
    )
    key_all = jnp.concatenate([kv_all[:, :half_k], kv_all[:, half_kv : half_kv + half_k]], axis=1)
    value_all = jnp.concatenate([kv_all[:, half_k:half_kv], kv_all[:, half_kv + half_k :]], axis=1)
    latent_low, query_rows = query_forward(latent_rows, query_full, gain_latent, shift_latent)
    mixed = attention_forward(meta, query_rows, key_all, value_all)
    result, act, middle_low, grad_hidden, grad_attn, grad_middle, grad_mixed, sums = middle_stage(
        used, mixed, latent_rows, grad_low, out_full, up_full, down_full, vecs
    )
    squares = total_of(jnp.sum(sums[:3], axis=1))
    valid_cells = float(docs * LAT * fsdp_count * D_LAT)
    rms_values = jnp.sqrt(squares / valid_cells)

    weight_grad = lambda left, right: dot_tn(left, right).astype(BF16)
    grad_w_down, grad_w_up, grad_w_out = reduce_halves(
        [weight_grad(act, grad_low), weight_grad(middle_low, grad_hidden), weight_grad(mixed, grad_attn)],
        place,
        core,
    )
    grad_query, grad_key, grad_value = attention_backward(
        meta, query_rows, key_all, value_all, grad_mixed
    )
    home = byte_rows.shape[0]
    grad_kv = jnp.concatenate(
        [grad_key[:, :half_k], grad_value[:, :half_v], grad_key[:, half_k:], grad_value[:, half_v:]],
        axis=1,
    )
    kept = lax.dynamic_slice_in_dim(grad_kv, core * home, home, axis=0)
    sent = lax.dynamic_slice_in_dim(grad_kv, (1 - core) * home, home, axis=0)
    grad_kv_home = own_sum(kept, swap_seq(sent))
    latent_grad, latent_sums = norm_backward_stage(
        "latent_backward", grad_query, query_full, latent_rows, gain_latent, grad_middle, LAT
    )
    byte_grad, byte_sums = norm_backward_stage(
        "byte_backward", grad_kv_home, kv_full, byte_rows, gain_bytes, None, 128
    )
    half_q = QK // 2
    grad_w_query = weight_grad(latent_low, grad_query).reshape(fsdp_count, lat_part, QK)
    grad_w_kv = weight_grad(byte_low, grad_kv_home).reshape(fsdp_count, byte_part, -1)
    rows8 = [byte_sums[0], byte_sums[1], latent_sums[0], latent_sums[1], sums[5], sums[6], sums[4], sums[3]]
    grad_table = jnp.stack(
        [
            jnp.pad(row.reshape(fsdp_count, -1), ((0, 0), (0, 128 - width)))
            for row, width in zip(rows8, widths)
        ],
        axis=1,
    ).astype(BF16)
    tall = max(lat_part, byte_part + 8)
    below = jnp.pad(grad_table, ((0, 0), (0, tall - byte_part - 8), (0, half_kv - 128)))
    grow = lambda v: jnp.pad(v, ((0, 0), (0, tall - lat_part), (0, 0)))
    first_grads = jnp.concatenate(
        [
            jnp.concatenate([grad_w_kv[:, :, :half_kv], below], axis=1),
            grow(grad_w_query[:, :, :half_q]),
            jnp.concatenate([grad_w_kv[:, :, half_kv:], jnp.zeros_like(below)], axis=1),
            grow(grad_w_query[:, :, half_q:]),
        ],
        axis=2,
    ).reshape(fsdp_count * tall, -1)
    ((low, high),) = reduce_halves([first_grads], place, core)
    pieces = [low[byte_part + i, :width] for i, width in enumerate(widths)]
    side = lambda pair: jnp.concatenate(pair, axis=1)
    grad_w_key = side((low[:byte_part, :half_k], high[:byte_part, :half_k]))
    grad_w_value = side((low[:byte_part, half_k:half_kv], high[:byte_part, half_k:half_kv]))
    grad_w_query = side((low[:lat_part, half_kv:], high[:lat_part, half_kv:]))
    return (
        result[None],
        latent_grad[None],
        byte_grad[None],
        pieces[0],
        pieces[1],
        pieces[2],
        pieces[3],
        pieces[4],
        pieces[5],
        grad_w_query,
        grad_w_key,
        grad_w_value,
        side(grad_w_out),
        side(grad_w_up),
        pieces[6],
        side(grad_w_down),
        pieces[7],
        rms_values,
    )


def solution(mesh):
    rows = P("fsdp", "seq", None)
    vec = P("fsdp")
    mat = P("fsdp", None)
    in_specs = (rows,) * 3 + (mat,) * 2 + (vec,) * 6 + (mat,) * 5 + (vec, mat, vec)
    out_specs = (rows,) * 3 + (vec,) * 6 + (mat,) * 5 + (vec, mat, vec, P())
    return jax.shard_map(shards, mesh=mesh, in_specs=in_specs, out_specs=out_specs, check_vma=False)
```

```python
import math

import jax
import jax.numpy as jnp
from jax import lax
from jax.experimental import pallas as pl
from jax.experimental.pallas import tpu as pltpu
from jax.sharding import PartitionSpec as P

D_LAT = 1280
D_BYTE = 768
HEADS = 8
QK = 256
LAT = 256
WIN = 128
EPSILON = 1e-05
NEG_FILL = -1e30
KEY_W = QK // HEADS
VAL_W = D_LAT // HEADS
SCALE = 1.0 / math.sqrt(KEY_W)
F32 = jnp.float32
BF16 = jnp.bfloat16


def dot_nn(a, b):
    return lax.dot_general(a, b, (((1,), (0,)), ((), ())), preferred_element_type=F32)


def dot_nt(a, b):
    return lax.dot_general(a, b, (((1,), (1,)), ((), ())), preferred_element_type=F32)


def dot_tn(a, b):
    return lax.dot_general(a, b, (((0,), (0,)), ((), ())), preferred_element_type=F32)


def params(mib=56):
    return pltpu.CompilerParams(
        dimension_semantics=("arbitrary",), vmem_limit_bytes=mib * 1024 * 1024
    )


def norm_parts(v):
    centred = v - jnp.mean(v, axis=-1, keepdims=True)
    inverse = lax.rsqrt(jnp.mean(centred * centred, axis=-1, keepdims=True) + EPSILON)
    return centred * inverse, inverse


def norm_back(upstream, hat, inverse, gain):
    scaled = upstream * gain
    centred = scaled - jnp.mean(scaled, axis=-1, keepdims=True)
    return inverse * (centred - hat * jnp.mean(scaled * hat, axis=-1, keepdims=True))


def colsum(v):
    return jnp.sum(v, axis=0, keepdims=True)


def whole(shape):
    return pl.BlockSpec(shape, lambda i, *_: (0,) * len(shape), pipeline_mode=pl.Buffered(1))


def rows_spec(rows, cols):
    return pl.BlockSpec((rows, cols), lambda i, *_: (i, 0))


def acc_spec(rows, cols):
    return pl.BlockSpec((rows, cols), lambda i, *_: (0, 0))


ANYWHERE = pl.BlockSpec(memory_space=pl.ANY)


def after(value, *others):
    return lax.optimization_barrier((value,) + others)[0]


def cost(flops, nbytes):
    return pl.CostEstimate(flops=int(flops), bytes_accessed=int(nbytes), transcendentals=0)


def byte_forward(byte_rows, w_kv, gain, shift):
    n = byte_rows.shape[0]
    blk = 128
    width = w_kv.shape[1]

    def body(x_ref, w_ref, g_ref, s_ref, low_ref, kv_ref):
        hat, _ = norm_parts(x_ref[...].astype(F32))
        low = (hat * g_ref[...] + s_ref[...]).astype(BF16)
        low_ref[...] = low
        kv_ref[...] = dot_nn(low, w_ref[...]).astype(BF16)

    return pl.pallas_call(
        body,
        name="byte_forward",
        grid=(n // blk,),
        in_specs=[rows_spec(blk, D_BYTE), whole(w_kv.shape), whole(gain.shape), whole(shift.shape)],
        out_specs=[rows_spec(blk, D_BYTE), rows_spec(blk, width)],
        out_shape=[
            jax.ShapeDtypeStruct((n, D_BYTE), BF16),
            jax.ShapeDtypeStruct((n, width), BF16),
        ],
        compiler_params=params(),
        cost_estimate=cost(2 * n * D_BYTE * width, 4e6),
    )(byte_rows, w_kv, gain, shift)


def query_forward(latents, w_q, gain, shift):
    n = latents.shape[0]

    def body(x_ref, w_ref, g_ref, s_ref, low_ref, q_ref):
        hat, _ = norm_parts(x_ref[...].astype(F32))
        low = (hat * g_ref[...] + s_ref[...]).astype(BF16)
        low_ref[...] = low
        q_ref[...] = dot_nn(low, w_ref[...]).astype(BF16)

    return pl.pallas_call(
        body,
        name="query_forward",
        grid=(n // LAT,),
        in_specs=[rows_spec(LAT, D_LAT), whole(w_q.shape), whole(gain.shape), whole(shift.shape)],
        out_specs=[rows_spec(LAT, D_LAT), rows_spec(LAT, QK)],
        out_shape=[jax.ShapeDtypeStruct((n, D_LAT), BF16), jax.ShapeDtypeStruct((n, QK), BF16)],
        compiler_params=params(),
        cost_estimate=cost(2 * n * D_LAT * QK, 1e7),
    )(latents, w_q, gain, shift)


def head_window(h):
    first = (h * VAL_W) // 128 * 128
    return first, h * VAL_W - first


def head_columns(x, low, width):
    col = lax.broadcasted_iota(jnp.int32, (1, x.shape[1]), 1)
    return jnp.where((col >= low) & (col < low + width), x, jnp.zeros((), x.dtype))


def load_keys_values(core, own_ref, twin_ref, k_ref, v_ref, sems):
    home = own_ref.shape[0]
    half_k, half_v = QK // 2, D_LAT // 2
    copies = []
    for which, ref in enumerate((own_ref, twin_ref)):
        row = pl.multiple_of((core ^ which) * home, 128)
        at = 0
        for half in range(2):
            for dest, width in ((k_ref, half_k), (v_ref, half_v)):
                copies.append(
                    pltpu.make_async_copy(
                        ref.at[:, at : at + width],
                        dest.at[pl.ds(row, home), half * width : (half + 1) * width],
                        sems.at[len(copies)],
                    )
                )
                at += width
    for copy in copies:
        copy.start()
    for copy in copies:
        copy.wait()


def attention_forward(meta, place, q, kv_own, kv_twin):
    n = q.shape[0]
    group = 2 * kv_own.shape[0]
    top = min(4, group // WIN)

    def body(meta_ref, place_ref, q_ref, own_ref, twin_ref, out_ref, acc_ref, k_ref, v_ref, sems):
        s = pl.program_id(0)

        @pl.when(s == 0)
        def _():
            load_keys_values(place_ref[3], own_ref, twin_ref, k_ref, v_ref, sems)

        first = meta_ref[0, s]
        count = meta_ref[1, s]
        lo = meta_ref[2, s]
        hi = meta_ref[3, s]

        @pl.when(count == 0)
        def _():
            out_ref[...] = jnp.zeros(out_ref.shape, BF16)

        def attend(w):
            at = pl.multiple_of(first, WIN)
            width = w * WIN
            pos = at + lax.broadcasted_iota(jnp.int32, (1, width), 1)
            allowed = (pos >= lo) & (pos < hi)
            qs = q_ref[...]
            kw = k_ref[pl.ds(at, width), :]
            acc_ref[...] = jnp.zeros(acc_ref.shape, F32)
            for h in range(HEADS):
                kh = head_columns(kw, h * KEY_W, KEY_W)
                scores = jnp.where(allowed, dot_nt(qs, kh) * SCALE, NEG_FILL)
                e = jnp.exp(scores - jnp.max(scores, axis=-1, keepdims=True))
                p = (e / jnp.sum(e, axis=-1, keepdims=True)).astype(BF16)
                base, off = head_window(h)
                vh = head_columns(v_ref[pl.ds(at, width), base : base + 256], off, VAL_W)
                acc_ref[:, base : base + 256] += dot_nn(p, vh)
            out_ref[...] = acc_ref[...].astype(BF16)

        for w in range(1, top + 1):
            pl.when(count == w)(lambda w=w: attend(w))

    return pl.pallas_call(
        body,
        name="attention_forward",
        grid_spec=pltpu.PrefetchScalarGridSpec(
            num_scalar_prefetch=2,
            grid=(n // LAT,),
            in_specs=[rows_spec(LAT, QK), ANYWHERE, ANYWHERE],
            out_specs=rows_spec(LAT, D_LAT),
            scratch_shapes=[
                pltpu.VMEM((LAT, D_LAT), F32),
                pltpu.VMEM((group, QK), BF16),
                pltpu.VMEM((group, D_LAT), BF16),
                pltpu.SemaphoreType.DMA((8,)),
            ],
        ),
        out_shape=jax.ShapeDtypeStruct((n, D_LAT), BF16),
        compiler_params=params(),
        cost_estimate=cost(4e9, 1e7),
    )(meta, place, q, kv_own, kv_twin)


def attention_backward(meta, place, q, kv_own, kv_twin, grad_mixed):
    n = q.shape[0]
    home, wide = kv_own.shape
    group = 2 * home
    half_k, half_v = QK // 2, D_LAT // 2
    top = min(4, group // WIN)
    steps = n // LAT

    def body(
        meta_ref, place_ref, q_ref, own_ref, twin_ref, gm_ref,
        gq_ref, kept_ref, sent_ref, gq_acc, gk_acc, gv_acc, k_ref, v_ref, sems,
    ):
        s = pl.program_id(0)
        first = meta_ref[0, s]
        count = meta_ref[1, s]
        lo = meta_ref[2, s]
        hi = meta_ref[3, s]

        @pl.when(s == 0)
        def _():
            load_keys_values(place_ref[3], own_ref, twin_ref, k_ref, v_ref, sems)
            gk_acc[...] = jnp.zeros(gk_acc.shape, F32)
            gv_acc[...] = jnp.zeros(gv_acc.shape, F32)

        @pl.when(count == 0)
        def _():
            gq_ref[...] = jnp.zeros(gq_ref.shape, BF16)

        def attend(w):
            at = pl.multiple_of(first, WIN)
            width = w * WIN
            pos = at + lax.broadcasted_iota(jnp.int32, (width, 1), 0)
            allowed = (pos >= lo) & (pos < hi)
            qs = q_ref[...]
            kw = k_ref[pl.ds(at, width), :]
            for h in range(HEADS):
                base, off = head_window(h)
                kh = head_columns(kw, h * KEY_W, KEY_W)
                scores = jnp.where(allowed, dot_nt(kh, qs) * SCALE, NEG_FILL)
                e = jnp.exp(scores - jnp.max(scores, axis=0, keepdims=True))
                p = e / jnp.sum(e, axis=0, keepdims=True)
                gm = head_columns(gm_ref[:, base : base + 256], off, VAL_W)
                gp = dot_nt(v_ref[pl.ds(at, width), base : base + 256], gm)
                inner = jnp.sum(p * gp, axis=0, keepdims=True)
                gs = (p * (gp - inner)).astype(BF16)
                gv_acc[pl.ds(at, width), base : base + 256] += dot_nn(p.astype(BF16), gm)
                gk_acc[pl.ds(at, width), :] += dot_nn(gs, head_columns(qs, h * KEY_W, KEY_W))
                part = dot_tn(gs, kh)
                if h == 0:
                    gq_acc[...] = part
                else:
                    gq_acc[...] += part
            gq_ref[...] = (gq_acc[...] * SCALE).astype(BF16)

        for w in range(1, top + 1):
            pl.when(count == w)(lambda w=w: attend(w))

        @pl.when(s == steps - 1)
        def _():
            for which, ref in enumerate((kept_ref, sent_ref)):
                row = pl.ds(pl.multiple_of((place_ref[3] ^ which) * home, 128), home)
                gk = (gk_acc[row, :] * SCALE).astype(BF16)
                gv = gv_acc[row, :].astype(BF16)
                ref[:, :half_k] = gk[:, :half_k]
                ref[:, half_k : half_k + half_v] = gv[:, :half_v]
                ref[:, half_k + half_v : wide - half_v] = gk[:, half_k:]
                ref[:, wide - half_v :] = gv[:, half_v:]

    return pl.pallas_call(
        body,
        name="attention_backward",
        grid_spec=pltpu.PrefetchScalarGridSpec(
            num_scalar_prefetch=2,
            grid=(steps,),
            in_specs=[rows_spec(LAT, QK), ANYWHERE, ANYWHERE, rows_spec(LAT, D_LAT)],
            out_specs=[rows_spec(LAT, QK), acc_spec(home, wide), acc_spec(home, wide)],
            scratch_shapes=[
                pltpu.VMEM((LAT, QK), F32),
                pltpu.VMEM((group, QK), F32),
                pltpu.VMEM((group, D_LAT), F32),
                pltpu.VMEM((group, QK), BF16),
                pltpu.VMEM((group, D_LAT), BF16),
                pltpu.SemaphoreType.DMA((8,)),
            ],
        ),
        out_shape=[
            jax.ShapeDtypeStruct((n, QK), BF16),
            jax.ShapeDtypeStruct((home, wide), BF16),
            jax.ShapeDtypeStruct((home, wide), BF16),
        ],
        compiler_params=params(),
        cost_estimate=cost(1e10, 1e7),
    )(meta, place, q, kv_own, kv_twin, grad_mixed)


ROOT_HALF = 1.0 / math.sqrt(2.0)
ROOT_2PI = 1.0 / math.sqrt(2.0 * math.pi)


def middle_stage(flags, place, mixed, latents, out_grad, weights, vecs):
    n = mixed.shape[0]
    count = len(weights)
    pieces = count == 10

    def body(flag_ref, place_ref, mix_ref, lat_ref, g_ref, vec_ref, *rest):
        weight_refs = rest[:count]
        (
            res_ref, act_ref, low_ref, gh_ref, ga_ref, gmid_ref, gmix_ref, sums_ref,
            wo_ref, wu_ref, wd_ref, sems,
        ) = rest[count:]
        i = pl.program_id(0)

        @pl.when(i == 0)
        def _():
            dests = (wo_ref, wu_ref, wd_ref)
            if pieces:
                jobs = [
                    (dest, m * (D_LAT // 2), D_LAT // 2, 0, weight_refs[0].shape[0] // 4)
                    for m, dest in enumerate(dests)
                ]
                copies = piece_copies(place_ref, weight_refs[:5], weight_refs[5:], jobs, sems)
            else:
                copies = [
                    pltpu.make_async_copy(src, dest, sems.at[m])
                    for m, (src, dest) in enumerate(zip(weight_refs, dests))
                ]
            for copy in copies:
                copy.start()
            for copy in copies:
                copy.wait()

        flag = flag_ref[i].astype(F32)
        mlp_gain = vec_ref[0:1, :]
        mlp_shift = vec_ref[1:2, :]
        up_bias = vec_ref[2:3, :]
        down_bias = vec_ref[3:4, :]
        attn = dot_nn(mix_ref[...], wo_ref[...])
        middle = lat_ref[...].astype(F32) + attn
        hat, inverse = norm_parts(middle)
        low = (hat * mlp_gain + mlp_shift).astype(BF16)
        low_ref[...] = low
        hidden = dot_nn(low, wu_ref[...]) + up_bias
        cdf = 0.5 * (1.0 + lax.erf(hidden * ROOT_HALF))
        pdf = jnp.exp(-0.5 * hidden * hidden) * ROOT_2PI
        act = (hidden * cdf).astype(BF16)
        act_ref[...] = act
        branch = dot_nn(act, wd_ref[...]) + down_bias
        result = middle + branch
        res_ref[...] = result.astype(BF16)
        g_low = g_ref[...]
        g = g_low.astype(F32)
        gh = (dot_nt(g_low, wd_ref[...]) * (cdf + hidden * pdf)).astype(BF16)
        gh_ref[...] = gh
        gmn = dot_nt(gh, wu_ref[...])
        gmid = g + norm_back(gmn, hat, inverse, mlp_gain)
        gmid_ref[...] = gmid
        ga = gmid.astype(BF16)
        ga_ref[...] = ga
        gmix_ref[...] = dot_nt(ga, wo_ref[...]).astype(BF16)

        @pl.when(i == 0)
        def _():
            sums_ref[...] = jnp.zeros(sums_ref.shape, F32)

        sums_ref[0:1, :] += flag * colsum(result * result)
        sums_ref[1:2, :] += flag * colsum(attn * attn)
        sums_ref[2:3, :] += flag * colsum(branch * branch)
        sums_ref[3:4, :] += colsum(g)
        sums_ref[4:5, :] += colsum(gh.astype(F32))
        sums_ref[5:6, :] += colsum(gmn * hat)
        sums_ref[6:7, :] += colsum(gmn)

    low_out = jax.ShapeDtypeStruct((n, D_LAT), BF16)
    blk = rows_spec(LAT, D_LAT)
    return pl.pallas_call(
        body,
        name="middle_stage",
        grid_spec=pltpu.PrefetchScalarGridSpec(
            num_scalar_prefetch=2,
            grid=(n // LAT,),
            in_specs=[blk, blk, blk, whole(vecs.shape)] + [ANYWHERE] * count,
            out_specs=[blk] * 7 + [acc_spec(8, D_LAT)],
            scratch_shapes=[pltpu.VMEM((D_LAT, D_LAT), BF16)] * 3
            + [pltpu.SemaphoreType.DMA((96,))],
        ),
        out_shape=[
            low_out, low_out, low_out, low_out, low_out,
            jax.ShapeDtypeStruct((n, D_LAT), F32),
            low_out,
            jax.ShapeDtypeStruct((8, D_LAT), F32),
        ],
        compiler_params=params(60),
        cost_estimate=cost(12 * n * D_LAT * D_LAT, 5e7),
    )(flags, place, mixed, latents, out_grad, vecs, *weights)


def norm_backward_stage(name, grad_rows, weight, rows, gain, extra, blk):
    n, d = rows.shape
    width = grad_rows.shape[1]
    has_extra = extra is not None

    def body(*refs):
        gr_ref, w_ref, x_ref, gain_ref = refs[:4]
        out_ref, sums_ref = refs[-2:]
        up = dot_nt(gr_ref[...], w_ref[...])
        hat, inverse = norm_parts(x_ref[...].astype(F32))
        back = norm_back(up, hat, inverse, gain_ref[...])
        if has_extra:
            back = back + refs[4][...]
        out_ref[...] = back.astype(BF16)

        @pl.when(pl.program_id(0) == 0)
        def _():
            sums_ref[...] = jnp.zeros(sums_ref.shape, F32)

        sums_ref[0:1, :] += colsum(up * hat)
        sums_ref[1:2, :] += colsum(up)

    operands = [grad_rows, weight, rows, gain] + ([extra] if has_extra else [])
    specs = [rows_spec(blk, width), whole(weight.shape), rows_spec(blk, d), whole(gain.shape)]
    return pl.pallas_call(
        body,
        name=name,
        grid=(n // blk,),
        in_specs=specs + ([rows_spec(blk, d)] if has_extra else []),
        out_specs=[rows_spec(blk, d), acc_spec(8, d)],
        out_shape=[jax.ShapeDtypeStruct((n, d), BF16), jax.ShapeDtypeStruct((8, d), F32)],
        compiler_params=params(),
        cost_estimate=cost(2 * n * d * width, 1e7),
    )(*operands)


def xor_pairs(count, bit):
    return [(i, i ^ bit) for i in range(count)]


def turn_pairs(count, plane, by):
    depth = count // plane
    return [(i, ((i // plane + by) % depth) * plane + i % plane) for i in range(count)]


def swap_seq(x):
    return lax.ppermute(x, "seq", [(0, 1), (1, 0)])


def stack_deep(pieces):
    r, c = pieces[0].shape

    def body(*refs):
        for k in range(4):
            refs[4][k * r : (k + 1) * r, :] = refs[k][...]

    return pl.pallas_call(
        body,
        name="stack_deep",
        grid=(1,),
        in_specs=[whole((r, c))] * 4,
        out_specs=pl.BlockSpec((4 * r, c), lambda i: (0, 0)),
        out_shape=jax.ShapeDtypeStruct((4 * r, c), BF16),
        compiler_params=params(),
        cost_estimate=cost(0, 16 * r * c),
    )(*pieces)


def piece_copies(place_ref, mine, other, jobs, sems):
    z, y, x, core = place_ref[0], place_ref[1], place_ref[2], place_ref[3]
    r = mine[0].shape[0] // 4
    copies = []
    for t in range(4):
        for k in range(4):
            chip = ((z + 4 - k) % 4) * 4 + (y ^ (t >> 1)) * 2 + (x ^ (t & 1))
            source, at = (t, k * r) if t < 3 else (3 + k // 2, (k % 2) * r)
            for which, refs in enumerate((mine, other)):
                for target, col, width, row, rows in jobs:
                    to_row = pl.multiple_of(chip * rows, 16)
                    to_col = pl.multiple_of((core ^ which) * width, 128)
                    copies.append(
                        pltpu.make_async_copy(
                            refs[source].at[at + row : at + row + rows, col : col + width],
                            target.at[pl.ds(to_row, rows), pl.ds(to_col, width)],
                            sems.at[len(copies)],
                        )
                    )
    return copies


def gather_columns(part):
    turn = lambda x, by: lax.ppermute(x, "fsdp", turn_pairs(16, 4, by))
    flip = lambda x, bit: lax.ppermute(x, "fsdp", xor_pairs(16, bit))
    r = part.shape[0]
    deep = stack_deep([part] + [turn(part, by) for by in (1, 2, 3)])
    by_x = flip(deep, 1)
    by_y = flip(deep, 2)
    far_x = flip(by_x[: 2 * r], 2)
    far_y = flip(by_y[2 * r :], 1)
    mine = [deep, by_x, by_y, far_x, far_y]
    return mine + [swap_seq(v) for v in mine]


def join_first(place, pieces, kv_rows, q_rows, wide_q):
    wide = pieces[0].shape[1]

    def body(place_ref, *refs):
        kv_ref, q_ref, table_ref, sems = refs[10:]
        jobs = [
            (kv_ref, 0, wide, 0, kv_rows),
            (q_ref, 0, wide_q, kv_rows, q_rows),
            (table_ref, wide_q, 128, kv_rows, q_rows),
        ]
        copies = piece_copies(place_ref, refs[:5], refs[5:10], jobs, sems)
        for copy in copies:
            copy.start()
        for copy in copies:
            copy.wait()

    shapes = [(16 * kv_rows, 2 * wide), (16 * q_rows, 2 * wide_q), (16 * q_rows, 256)]
    return pl.pallas_call(
        body,
        name="join_first",
        grid_spec=pltpu.PrefetchScalarGridSpec(
            num_scalar_prefetch=1,
            grid=(1,),
            in_specs=[ANYWHERE] * 10,
            out_specs=[pl.BlockSpec(shape, lambda i, *_: (0, 0)) for shape in shapes],
            scratch_shapes=[pltpu.SemaphoreType.DMA((96,))],
        ),
        out_shape=[jax.ShapeDtypeStruct(shape, BF16) for shape in shapes],
        compiler_params=params(),
        cost_estimate=cost(0, 8e6),
    )(place, *pieces)


def gather_parameters(place, core, kv_halves, w_query, vectors, squares):
    table = jnp.stack([jnp.pad(v, (0, 128 - v.shape[0])) for v in vectors])
    if lax.axis_size("fsdp") != 16:
        take = lambda v: lax.all_gather(v, "fsdp", axis=0, tiled=True)
        whole_table = take(table).reshape(-1, 8, 128).astype(F32)
        return take(jnp.concatenate(kv_halves, axis=1)), take(w_query), whole_table, [
            take(w) for w in squares
        ]
    half_q = QK // 2
    q_rows = 16
    wide_q = w_query.shape[0] * half_q // q_rows
    kv_part = jnp.where(core == 0, kv_halves[0], kv_halves[1])
    q_part = jnp.where(core == 0, w_query[:, :half_q], w_query[:, half_q:])
    below = jnp.concatenate(
        [q_part.reshape(q_rows, wide_q), jnp.pad(table, ((0, q_rows - 8), (0, 0)))], axis=1
    )
    first = gather_columns(jnp.concatenate([kv_part, below], axis=0))
    half = squares[0].shape[1] // 2
    own_part = jnp.concatenate(
        [jnp.where(core == 0, w[:, :half], w[:, half:]) for w in squares], axis=1
    )
    second = gather_columns(after(own_part, first[0]))
    kv_full, query_rows, tables = join_first(place, first, kv_part.shape[0], q_rows, wide_q)
    per_row = wide_q // half_q
    query_full = query_rows.reshape(16, q_rows, 2, per_row, half_q)
    query_full = query_full.transpose(0, 1, 3, 2, 4).reshape(-1, QK)
    return kv_full, query_full, tables.reshape(16, q_rows, 256)[:, :8, :128].astype(F32), second


def own_sum(kept, arrived):
    return (kept.astype(F32) + arrived.astype(F32)).astype(BF16)


def pick(v, i, axis):
    return lax.dynamic_index_in_dim(v, i, axis, keepdims=False)


def reduce_begin(kept, sent):
    return jnp.stack([own_sum(k, swap_seq(s)) for k, s in zip(kept, sent)])


def reduce_split(half, place):
    y, x = place[1], place[2]
    m, rows, c = half.shape
    blocks = half.reshape(m, 4, 2, 2, rows // 16, c)
    a, b = blocks[:, :2], blocks[:, 2:]
    return pick(a, x, 3), pick(a, 1 - x, 3), pick(b, y, 2), pick(b, 1 - y, 2)


def reduce_next(parts, place):
    y, x = place[1], place[2]
    a_kept, a_sent, b_kept, b_sent = parts
    a = own_sum(a_kept, lax.ppermute(a_sent, "fsdp", xor_pairs(16, 1)))
    b = own_sum(b_kept, lax.ppermute(b_sent, "fsdp", xor_pairs(16, 2)))
    return pick(a, y, 2), pick(a, 1 - y, 2), pick(b, x, 2), pick(b, 1 - x, 2)


def reduce_depth(parts, place):
    z = place[0]
    a_kept, a_sent, b_kept, b_sent = parts
    a = own_sum(a_kept, lax.ppermute(a_sent, "fsdp", xor_pairs(16, 2)))
    b = own_sum(b_kept, lax.ppermute(b_sent, "fsdp", xor_pairs(16, 1)))
    deep = jnp.concatenate([a, b], axis=1)
    return [pick(deep, (z + by) % 4, 1) for by in range(4)]


def reduce_end(pieces, core):
    total = pieces[0].astype(F32)
    for by in (1, 2, 3):
        total = total + lax.ppermute(pieces[by], "fsdp", turn_pairs(16, 4, by)).astype(F32)
    return share_halves(total.astype(BF16), core)


def share_halves(shard, core):
    twin = swap_seq(shard)
    low = jnp.where(core == 0, shard, twin).astype(F32)
    high = jnp.where(core == 0, twin, shard).astype(F32)
    return low, high


def reduce_plain(half, core):
    return share_halves(lax.psum_scatter(half, "fsdp", scatter_dimension=1, tiled=True), core)


def total_of(values):
    if lax.axis_size("fsdp") != 16:
        return lax.psum(values, ("seq", "fsdp"))
    values = values + swap_seq(values)
    for bit in (1, 2, 4, 8):
        values = values + lax.ppermute(values, "fsdp", xor_pairs(16, bit))
    return values


def shards(
    byte_stream,
    latents,
    out_grad,
    doc_lengths,
    slot_ids,
    byte_gain,
    byte_shift,
    latent_gain,
    latent_shift,
    mlp_gain,
    mlp_shift,
    w_query,
    w_key,
    w_value,
    w_out,
    w_up,
    up_bias,
    w_down,
    down_bias,
):
    seq_count = lax.axis_size("seq")
    fsdp_count = lax.axis_size("fsdp")
    core = lax.axis_index("seq")
    chip = lax.axis_index("fsdp")
    place = jnp.stack([chip // 4, (chip // 2) % 2, chip % 2, core]).astype(jnp.int32)

    byte_part = byte_gain.shape[0]
    lat_part = latent_gain.shape[0]
    half_k, half_v = QK // 2, D_LAT // 2
    half_kv = half_k + half_v
    kv_halves = [
        jnp.concatenate([w_key[:, :half_k], w_value[:, :half_v]], axis=1),
        jnp.concatenate([w_key[:, half_k:], w_value[:, half_v:]], axis=1),
    ]
    kv_full, query_full, table, squares_full = gather_parameters(
        place,
        core,
        kv_halves,
        w_query,
        (byte_gain, byte_shift, latent_gain, latent_shift, mlp_gain, mlp_shift, up_bias, down_bias),
        (w_out, w_up, w_down),
    )
    widths = (byte_part, byte_part) + (lat_part,) * 6
    vectors = [table[:, i, :width].reshape(1, -1) for i, width in enumerate(widths)]
    gain_bytes, shift_bytes, gain_latent, shift_latent = vectors[:4]
    bias_down = vectors[7]
    vecs = jnp.concatenate(vectors[4:] + [bias_down] * 4, axis=0)

    lengths = doc_lengths[0]
    docs = lengths.shape[0]
    slots = slot_ids.shape[1] // seq_count
    ends = jnp.cumsum(lengths)
    own_slots = core * slots + jnp.arange(slots, dtype=jnp.int32)
    hit = (slot_ids[0, :docs][None, :] == own_slots[:, None]).astype(jnp.int32)
    lo = jnp.sum(hit * (ends - lengths)[None, :], axis=1)
    hi = jnp.sum(hit * ends[None, :], axis=1)
    used = jnp.sum(hit, axis=1)
    base = lo // WIN * WIN
    meta = jnp.stack([base, used * ((hi - base + WIN - 1) // WIN), lo, hi]).astype(jnp.int32)

    byte_rows = byte_stream[0]
    latent_rows = latents[0]
    grad_low = out_grad[0]
    byte_low, kv_rows = byte_forward(byte_rows, kv_full, gain_bytes, shift_bytes)
    kv_twin = swap_seq(kv_rows)
    latent_low, query_rows = query_forward(latent_rows, query_full, gain_latent, shift_latent)
    mixed = attention_forward(meta, place, query_rows, kv_rows, kv_twin)
    result, act, middle_low, grad_hidden, grad_attn, grad_middle, grad_mixed, sums = middle_stage(
        used, place, mixed, latent_rows, grad_low, squares_full, vecs
    )

    staged = fsdp_count == 16
    half = D_LAT // 2
    weight_grad = lambda left, right: dot_tn(left, right).astype(BF16)
    columns = lambda v, which: lax.dynamic_slice_in_dim(v, which * half, half, axis=1)
    pairs = [(act, grad_low), (middle_low, grad_hidden), (mixed, grad_attn)]
    sent = [weight_grad(left, columns(right, 1 - core)) for left, right in pairs]
    kept = [weight_grad(left, columns(right, core)) for left, right in pairs]
    square_half = reduce_begin(kept, sent)
    if staged:
        square_parts = reduce_split(square_half, place)
        grad_mixed = after(grad_mixed, square_parts[1], square_parts[3])
    grad_query, kv_kept, kv_sent = attention_backward(
        meta, place, query_rows, kv_rows, kv_twin, grad_mixed
    )
    grad_kv_home = own_sum(kv_kept, swap_seq(kv_sent))
    if staged:
        square_parts = reduce_next(square_parts, place)
        grad_query = after(grad_query, square_parts[1], square_parts[3])
    half_q = QK // 2
    grad_w_query = weight_grad(latent_low, grad_query)
    grad_w_kv = weight_grad(byte_low, grad_kv_home)
    query_ahead = grad_query
    if staged:
        q_rows = 16
        halves = []
        for which in range(2):
            q_half = grad_w_query[:, which * half_q : (which + 1) * half_q]
            q_half = q_half.reshape(fsdp_count, q_rows, -1)
            q_half = jnp.pad(q_half, ((0, 0), (0, 0), (0, half_kv - q_half.shape[2])))
            kv_half = grad_w_kv[:, which * half_kv : (which + 1) * half_kv]
            kv_half = kv_half.reshape(fsdp_count, byte_part, half_kv)
            halves.append(jnp.concatenate([kv_half, q_half], axis=1).reshape(-1, half_kv))
        first_sent = jnp.where(core == 0, halves[1], halves[0])
        first_kept = jnp.where(core == 0, halves[0], halves[1])
        query_ahead = after(grad_query, first_sent)
    latent_grad, latent_sums = norm_backward_stage(
        "latent_backward", query_ahead, query_full, latent_rows, gain_latent, grad_middle, LAT
    )
    kv_ahead = grad_kv_home
    if staged:
        first_parts = reduce_split(reduce_begin([first_kept], [first_sent]), place)
        square_deep = reduce_depth(square_parts, place)
        kv_ahead = after(grad_kv_home, first_parts[1], first_parts[3], *square_deep[1:])
    byte_grad, byte_sums = norm_backward_stage(
        "byte_backward", kv_ahead, kv_full, byte_rows, gain_bytes, None, 128
    )
    if staged:
        first_low, first_high = reduce_end(
            reduce_depth(reduce_next(first_parts, place), place), core
        )
        square_low, square_high = reduce_end(square_deep, core)
        kv_low, kv_high = first_low[0, :byte_part], first_high[0, :byte_part]
        per_shard = lambda v: v[0, byte_part:, : lat_part * half_q // q_rows].reshape(lat_part, half_q)
        q_low, q_high = per_shard(first_low), per_shard(first_high)
    else:
        split = lambda v, c: ([jnp.where(core == 0, v[:, :c], v[:, c:])], [jnp.where(core == 0, v[:, c:], v[:, :c])])
        square_low, square_high = reduce_plain(square_half, core)
        (kv_low,), (kv_high,) = reduce_plain(reduce_begin(*split(grad_w_kv, half_kv)), core)
        (q_low,), (q_high,) = reduce_plain(reduce_begin(*split(grad_w_query, half_q)), core)
    side = lambda low, high: jnp.concatenate([low, high], axis=1)
    grad_w_key = side(kv_low[:, :half_k], kv_high[:, :half_k])
    grad_w_value = side(kv_low[:, half_k:], kv_high[:, half_k:])
    grad_w_down, grad_w_up, grad_w_out = [side(square_low[m], square_high[m]) for m in range(3)]

    byte_cols = jnp.pad(byte_sums[:2], ((0, 0), (0, D_LAT - D_BYTE)))
    totals = total_of(jnp.concatenate([sums[:7], latent_sums[:2], byte_cols], axis=0))
    valid_cells = float(docs * LAT * fsdp_count * D_LAT)
    rms_values = jnp.sqrt(jnp.sum(totals[:3], axis=1) / valid_cells)
    own = lambda row, width: lax.dynamic_slice_in_dim(totals[row], chip * width, width, axis=0)
    order = (9, 10, 7, 8, 5, 6, 4, 3)
    pieces = [own(row, width) for row, width in zip(order, widths)]
    return (
        result[None],
        latent_grad[None],
        byte_grad[None],
        pieces[0],
        pieces[1],
        pieces[2],
        pieces[3],
        pieces[4],
        pieces[5],
        side(q_low, q_high),
        grad_w_key,
        grad_w_value,
        grad_w_out,
        grad_w_up,
        pieces[6],
        grad_w_down,
        pieces[7],
        rms_values,
    )


def solution(mesh):
    rows = P("fsdp", "seq", None)
    vec = P("fsdp")
    mat = P("fsdp", None)
    in_specs = (rows,) * 3 + (mat,) * 2 + (vec,) * 6 + (mat,) * 5 + (vec, mat, vec)
    out_specs = (rows,) * 3 + (vec,) * 6 + (mat,) * 5 + (vec, mat, vec, P())
    return jax.shard_map(shards, mesh=mesh, in_specs=in_specs, out_specs=out_specs, check_vma=False)
```
